32 devices in a mesh: grp: 8 (over y, x, core), head: 4 (over z).
Axes of the slice: x: 2, y: 2, z: 4, core: 2. Of those that a mesh axis runs over, the one named last changes fastest.
Arguments:
- q_nope: bfloat16 [4, 64, 128, 128], P(None, 'grp', 'head'), may hold values from -6 to 6
- q_rope: bfloat16 [4, 64, 128, 64], P(None, 'grp', 'head'), may hold values from -512 to 512
- w_absorb_k: bfloat16 [128, 128, 512], P('head'), may hold values from -0.5 to 0.5
- w_absorb_v: bfloat16 [128, 512, 128], P('head'), may hold values from -0.25 to 0.25
- latent_cache: bfloat16 [64, 1024, 576], P(('grp', 'head')), may hold values from -4 to 4
- new_latent: bfloat16 [4, 64, 576], P(None, ('grp', 'head')), may hold values from -6 to 6
- lengths: int32 [64], replicated, may hold values from 128 to 1020, as said below
- moves: int32 [4, 1], P('head'), may hold values from 1 to 7
Outputs:
- attended: bfloat16 [4, 64, 128, 128], P(None, 'grp', 'head')
The draws below stay inside these ranges and needn't reach their ends.
Inputs may be any that keep to these rules, and one draw needn't show every extreme that they name: lengths[r] counts the live rows of latent_cache[r]; its later rows up to 1024 are padding that no query reads.
All inputs are finite; a program needn't handle non-finite values.
Results may differ from the reference program's by a relative error of at most 0.0077.
Values may be sent and summed in bfloat16 or wider, within the bound.
A program may use at most 64 MiB of HBM per device.

```python
import math
import jax
import jax.numpy as jnp
from jax import lax

HEADS = 128
HEAD_DIM = 128
ROPE = 64
LATENT = 512
BLOCK = 128
STEPS = 4
REQ_DEV = 2
KV = 576
CAP = 1024
MOVERS = 1
GROUPS = 8
COLUMNS = 4
REQUESTS = 64


def first_keys(key):
    return jax.random.truncated_normal(jax.random.fold_in(key, 8), -4.0, 4.0, (REQUESTS, ROPE), jnp.float32)


def draw_latent_cache(key, part):
    shape = (REQUESTS, CAP, LATENT + ROPE)
    values = jax.random.truncated_normal(jax.random.fold_in(key, 7), -4.0, 4.0, shape, jnp.float32)
    values = values.at[:, 0, LATENT:].set(first_keys(key))
    return values.astype(jnp.bfloat16)


def draw_q_rope(key, part):
    shape = (STEPS, REQUESTS, HEADS, ROPE)
    values = jax.random.truncated_normal(jax.random.fold_in(key, 11), -4.0, 4.0, shape, jnp.float32)
    return values.astype(jnp.bfloat16)


def draw_lengths(key, part):
    spread_top = CAP - STEPS - BLOCK
    factor_one = jax.random.randint(jax.random.fold_in(key, 21), (REQUESTS,), 0, spread_top + 1)
    factor_two = jax.random.randint(jax.random.fold_in(key, 22), (REQUESTS,), 0, spread_top + 1)
    values = BLOCK + factor_one * factor_two // spread_top
    shuffled = jax.random.permutation(jax.random.fold_in(key, 23), REQUESTS)
    values = values.at[shuffled[0]].set(CAP - STEPS).at[shuffled[1]].set(BLOCK)
    return values.astype(jnp.int32)


def draw_moves(key, part):
    values = jax.random.randint(jax.random.fold_in(key, 31), (COLUMNS, MOVERS), 1, GROUPS)
    forced_at = jax.random.randint(jax.random.fold_in(key, 32), (), 0, COLUMNS * MOVERS)
    flattened = values.reshape(-1).at[forced_at].set(GROUPS - 1)
    return flattened.reshape(COLUMNS, MOVERS).astype(jnp.int32)


def block_scale(stream_key, dims, pieces, low, high):
    def one(dim, shards_of):
        draws = jax.random.uniform(jax.random.fold_in(jax.random.fold_in(stream_key, 6), dim), (shards_of,), jnp.float32, low / len(pieces), high / len(pieces))
        return jnp.repeat(jnp.exp(draws), dims[dim] // shards_of).reshape((-1,) + (1,) * (len(dims) - dim - 1))

    factor_of = one(*pieces[0])
    for cut in pieces[1:]:
        factor_of = factor_of * one(*cut)
    return factor_of


def normal_values(rng, dims, width, most, cuts=(), kind=jnp.bfloat16):
    result = width * jax.random.normal(rng, dims, jnp.float32)
    if cuts:
        result = result * block_scale(rng, dims, cuts, -0.22, 0.18)
    return jnp.clip(result, -most, most).astype(kind)


def setup_inputs(seed: int = 0) -> dict:
    splits = jax.random.split(jax.random.key(seed), 9)
    return {
        "q_nope": normal_values(splits[0], (STEPS, REQUESTS, HEADS, HEAD_DIM), 1.0, 6.0, ((1, 8), (2, 4))),
        "q_rope": draw_q_rope(jax.random.fold_in(splits[8], 71), 0),
        "w_absorb_k": normal_values(splits[2], (HEADS, HEAD_DIM, LATENT), HEAD_DIM ** -0.5, 0.5, ((0, 4),)),
        "w_absorb_v": normal_values(splits[3], (HEADS, LATENT, HEAD_DIM), LATENT ** -0.5, 0.25, ((0, 4),)),
        "latent_cache": draw_latent_cache(jax.random.fold_in(splits[8], 71), 0),
        "new_latent": normal_values(splits[5], (STEPS, REQUESTS, KV), 1.0, 6.0, ((1, 32),)),
        "lengths": draw_lengths(jax.random.fold_in(splits[8], 71), 0),
        "moves": draw_moves(jax.random.fold_in(splits[8], 71), 0),
    }


yarn_gain = (0.1 * math.log(40.0) + 1.0) ** 2

def home_slots(moves):
    group_ids = jnp.arange(GROUPS, dtype=jnp.int32)[:, None, None]
    column_ids = jnp.arange(COLUMNS, dtype=jnp.int32)[None, :, None]
    place_ids = jnp.arange(REQ_DEV, dtype=jnp.int32)[None, None, :]
    offsets = jnp.concatenate([moves.astype(jnp.int32), jnp.zeros((COLUMNS, REQ_DEV - MOVERS), jnp.int32)], axis=1)[None, :, :]
    source = jnp.mod(group_ids - offsets, GROUPS)
    return ((source * COLUMNS + column_ids) * REQ_DEV + place_ids).reshape(-1).astype(jnp.int32)

def attend_one(query_row, stored, live_count, recent, live_steps, score_scale):
    query_wide = query_row.astype(jnp.float32)
    scores = jnp.einsum('hc,tc->ht', query_wide, stored.astype(jnp.float32)) * score_scale
    positions = jnp.arange(stored.shape[0], dtype=jnp.int32)
    scores = jnp.where(positions[None, :] < live_count, scores, -jnp.inf)
    extra_scores = jnp.einsum('hc,jc->hj', query_wide, recent.astype(jnp.float32)) * score_scale
    extra_scores = jnp.where(live_steps[None, :], extra_scores, -jnp.inf)
    peak = jnp.maximum(lax.optimization_barrier(jnp.max(scores, axis=1)), lax.optimization_barrier(jnp.max(extra_scores, axis=1)))[:, None]
    spread = jnp.exp(scores - peak)
    spread_new = jnp.exp(extra_scores - peak)
    softmax_sum = lax.optimization_barrier(jnp.sum(spread, axis=1, keepdims=True)) + lax.optimization_barrier(jnp.sum(spread_new, axis=1, keepdims=True))
    weights = lax.optimization_barrier((spread / softmax_sum).astype(jnp.bfloat16)).astype(jnp.float32)
    weights_new = lax.optimization_barrier((spread_new / softmax_sum).astype(jnp.bfloat16)).astype(jnp.float32)
    mixed_rows = jnp.einsum('ht,tl->hl', weights, stored[:, :LATENT].astype(jnp.float32))
    mixed_rows = mixed_rows + jnp.einsum('hj,jl->hl', weights_new, recent[:, :LATENT].astype(jnp.float32))
    return mixed_rows.astype(jnp.bfloat16)

def reference(q_nope, q_rope, w_absorb_k, w_absorb_v, latent_cache, new_latent, lengths, moves):
    score_scale = yarn_gain / math.sqrt(HEAD_DIM + ROPE)
    own_rows = jnp.arange(REQUESTS, dtype=jnp.int32)
    moved_rows = home_slots(moves)
    batch_rows = COLUMNS * REQ_DEV
    step_ids = jnp.arange(STEPS, dtype=jnp.int32)
    results = []
    for moment in range(STEPS):
        home_rows = moved_rows if moment >= 2 else own_rows
        root = jnp.where(step_ids[None, :] < 2, home_rows[:, None], own_rows[:, None]).astype(jnp.int32)
        live_steps = step_ids <= moment
        q_latent = jnp.einsum('rhd,hdl->rhl', q_nope[moment].astype(jnp.float32), w_absorb_k.astype(jnp.float32)).astype(jnp.bfloat16)
        queries = jnp.concatenate([q_latent, q_rope[moment]], axis=2)

        def one_block(element):
            block_queries, block_home, block_root = element

            def one_request(query_row, source, chosen_rows):
                stored = lax.dynamic_index_in_dim(latent_cache, source, 0, keepdims=False)
                recent = new_latent[step_ids, chosen_rows]
                live_count = lengths[source]
                return attend_one(query_row, stored, live_count, recent, live_steps, score_scale)
            return jax.vmap(one_request)(block_queries, block_home, block_root)
        mixed_rows = lax.map(one_block, (queries.reshape(-1, batch_rows, HEADS, queries.shape[2]), home_rows.reshape(-1, batch_rows), root.reshape(-1, batch_rows, STEPS)))
        mixed_rows = mixed_rows.reshape(REQUESTS, HEADS, LATENT)
        results.append(jnp.einsum('rhl,hld->rhd', mixed_rows.astype(jnp.float32), w_absorb_v.astype(jnp.float32)).astype(jnp.bfloat16))
    return jnp.stack(results)
```

```python
import functools
import math

import jax
import jax.numpy as jnp
from jax import lax
from jax.experimental import pallas as pl
from jax.experimental.pallas import tpu as pltpu
from jax.sharding import PartitionSpec as P

PAIR = 2
EXTRA = 128
LANES = 128
YARN_GAIN = (0.1 * math.log(40.0) + 1.0) ** 2
MESH = pl.DeviceIdType.MESH


def lane(c):
    return slice(c * LANES, (c + 1) * LANES)


def rounded(value):
    return value.astype(jnp.bfloat16)


def wide(value):
    return value.astype(jnp.float32)


def kernel(
    groups, columns, scale,
    length_hbm, move_ref, nope_hbm, rope_hbm, fresh_hbm, wk_hbm, wv_hbm, cache_hbm,
    out_ref,
    length_ref, nope_ref, rope_ref, fresh_ref, entry_sem,
    wk, wv, keys, newer, local_sem,
    rows_in, rows_mid, rows_out,
    lat_send, lat_recv, rot_send, rot_recv, back_send, back_recv,
    mine, moved, mine_key, moved_key, home, home_recv, shift_of, shift_mine,
    lat_ss, lat_rs, rot_ss, rot_rs, back_ss, back_rs,
    mine_ss, mine_rs, key_ss, key_rs, home_ss, home_rs, shift_ss, shift_rs,
    plane_sem, open_sem,
):
    steps, _, heads, _ = nope_ref.shape
    holders, entries, capacity = cache_hbm.shape
    latent = wk.shape[2]
    rope = entries - latent
    movers = move_ref.shape[1]
    total = capacity + EXTRA
    cuts = lat_ss.shape[2]
    cut = heads // cuts
    rank = lax.axis_index("grp")
    column = lax.axis_index("head")
    parts = wk.shape[0] // local_part(heads)
    part = local_part(heads)
    hub = min(1, columns - 1)

    first = [(0, k) for k in range(holders)]
    rest = [(1, k) for k in range(movers, holders)]
    moving = [(1, k) for k in range(movers)]
    settled = first + rest
    number = {member: u for u, member in enumerate(settled + moving)}

    def at_column(e):
        return (rank, lax.rem(column + e + columns, columns))

    def at_group(d):
        return (lax.rem(rank + d + groups, groups), column)

    barrier = pltpu.get_barrier_semaphore()
    for e in range(1, columns):
        pl.semaphore_signal(barrier, inc=1, device_id=at_column(e), device_id_type=MESH)

    @pl.when(column == hub)
    def _():
        for d in range(1, groups):
            pl.semaphore_signal(barrier, inc=1, device_id=at_group(d), device_id_type=MESH)

    wk_copies = [
        pltpu.make_async_copy(
            wk_hbm.at[pl.ds(n * part, part)], wk.at[pl.ds(n * part, part)], local_sem.at[n]
        )
        for n in range(parts)
    ]
    key_copies = [
        pltpu.make_async_copy(
            cache_hbm.at[k], keys.at[k], local_sem.at[parts + k]
        )
        for k in range(holders)
    ]
    wv_copy = pltpu.make_async_copy(wv_hbm, wv, local_sem.at[parts + holders])
    entry_copies = [
        pltpu.make_async_copy(src, dst, entry_sem.at[n])
        for n, (src, dst) in enumerate(
            (
                (rope_hbm, rope_ref), (nope_hbm, nope_ref), (fresh_hbm, fresh_ref),
                (length_hbm, length_ref),
            )
        )
    ]
    for copy in entry_copies[:2] + wk_copies + entry_copies[2:]:
        copy.start()

    def remote(src, dst, send, recv, target):
        return pltpu.make_async_remote_copy(
            src_ref=src, dst_ref=dst, send_sem=send, recv_sem=recv,
            device_id=target, device_id_type=MESH,
        )

    sent = []

    def launch(copy):
        copy.start()
        sent.append(copy)

    def slot(e, k):
        return lax.rem(column + e, columns) * holders + k

    def turned(span, e, k):
        return jnp.concatenate(
            [rope_ref[span * PAIR + s, slot(e, k)] for s in range(PAIR)], axis=1
        )

    shift_copies = [
        remote(shift_mine, shift_of.at[e], shift_ss.at[e], shift_rs.at[e], at_column(-e))
        for e in range(1, columns)
    ]
    mine_copies = [
        remote(mine, moved.at[d - 1], mine_ss.at[d - 1], mine_rs.at[d - 1], at_group(-d))
        for d in range(1, groups)
    ]
    newer_copies = [
        remote(mine_key, moved_key.at[d - 1], key_ss.at[d - 1], key_rs.at[d - 1], at_group(-d))
        for d in range(1, groups)
    ]
    home_copies = [
        remote(home, home_recv.at[d - 1], home_ss.at[d - 1], home_rs.at[d - 1], at_group(d))
        for d in range(1, groups)
    ]

    per = PAIR * cut

    def lat_copy(member, e, c):
        u = number[member]
        at = pl.ds(c * per, per) if member == first[0] else pl.ds(0, PAIR * heads)
        return remote(
            lat_send.at[u, e, at], lat_recv.at[u, e, at], lat_ss.at[u, e, c], lat_rs.at[u, e, c],
            at_column(e),
        )

    def lat_pieces(member):
        return cuts if member == first[0] else 1

    def rot_copy(late, e):
        at = pl.ds(len(settled), len(moving)) if late else pl.ds(0, len(settled))
        return remote(
            rot_send.at[e, at], rot_recv.at[e, at], rot_ss.at[late, e], rot_rs.at[late, e],
            at_column(e),
        )

    def back_copy(member, e, c):
        u = number[member]
        at = pl.ds(c * per, per) if member in rest else pl.ds(0, PAIR * heads)
        return remote(
            back_send.at[u, e, at], back_recv.at[u, e, at], back_ss.at[u, e, c],
            back_rs.at[u, e, c], at_column(-e),
        )

    def back_pieces(member):
        return cuts if member in rest else 1

    low, high = jnp.int32(0), jnp.int32(columns - 1)
    upward, downward = [], []
    for _ in range(columns - 1):
        take_high = high - column >= column - low
        target = jnp.where(take_high, high, low)
        upward.append(lax.rem(target - column + columns, columns))
        downward.append(lax.rem(column - target + columns, columns))
        high = jnp.where(take_high, high - 1, high)
        low = jnp.where(take_high, low, low + 1)

    def chosen(e, k, options):
        found = wide(options(0))
        for d in range(2, groups):
            is_it = shift_of[e, k, 0:1, 0:1] == d
            found = jnp.where(is_it, wide(options(d - 1)), found)
        return found

    unit_rows = columns * PAIR * heads

    def place(m, e, s):
        return ((m * columns + e) * PAIR + s) * heads

    def turn(members, late):
        for span, k in members:
            u = number[span, k]
            for e in range(columns):
                if late:
                    pair = rounded(chosen(e, k, lambda n: moved[n, k, PAIR, e]))
                else:
                    pair = turned(span, e, k)
                if e:
                    rot_send[e, u] = pair
                else:
                    rot_recv[0, u] = pair

    def absorb(members, begin, late, between):
        count = len(members) * columns * PAIR
        for m, (span, k) in enumerate(members):
            for e in range(columns):
                for s in range(PAIR):
                    if late:
                        value = chosen(e, k, lambda n: moved[n, k, s, e])
                    else:
                        value = wide(nope_ref[span * PAIR + s, slot(e, k)])
                    rows_in[pl.ds(place(m, e, s), heads)] = value
        for n in range(parts):
            if not late:
                wk_copies[n].wait()

            def head(i, carry):
                picked = rounded(rows_in[pl.ds(i, count, stride=heads)])
                result = jnp.dot(picked, wk[i], preferred_element_type=jnp.float32)
                for c in range(latent // LANES):
                    rows_mid[c, pl.ds(i, count, stride=heads)] = result[:, lane(c)]
                return carry

            lax.fori_loop(n * part, (n + 1) * part, head, 0, unroll=True)
            if (n + 1) % (parts // cuts):
                continue
            c = n // (parts // cuts)
            for m, member in enumerate(members):
                u = number[member]
                for e in range(columns):
                    value = jnp.concatenate(
                        [
                            jnp.concatenate(
                                [
                                    rounded(rows_mid[l, pl.ds(place(m, e, s) + c * cut, cut)])
                                    for l in range(latent // LANES)
                                ],
                                axis=1,
                            )
                            for s in range(PAIR)
                        ],
                        axis=0,
                    )
                    if e:
                        lat_send[u, e, c * per : (c + 1) * per] = value
                    else:
                        lat_recv[u, 0, c * per : (c + 1) * per] = value
                if member in begin and (member == first[0] or c == cuts - 1):
                    for e in upward:
                        launch(lat_copy(member, e, c if lat_pieces(member) > 1 else 0))
            between(c)

    entry_copies[0].wait()
    turn(settled, 0)
    pl.semaphore_wait(
        barrier, jnp.where(column == hub, columns - 1 + groups - 1, columns - 1)
    )

    @pl.when(column == hub)
    def _():
        for d in range(1, groups):
            pl.semaphore_signal(plane_sem, inc=1, device_id=at_group(d), device_id_type=MESH)

    for e in upward:
        launch(rot_copy(0, e))
    for copy in entry_copies[1:]:
        copy.wait()
    row = lax.broadcasted_iota(jnp.int32, (16, entries), 0)

    def fresh_rows(k):
        found = jnp.zeros((16, entries), jnp.float32)
        for j in range(steps):
            found = jnp.where(row == j, wide(fresh_ref[j])[k : k + 1], found)
        return found

    def between(c):
        if c == 0:
            for k in range(movers):
                for e in range(columns):
                    for s in range(PAIR):
                        mine[k, s, e] = nope_ref[PAIR + s, slot(e, k)]
                    mine[k, PAIR, e] = turned(1, e, k)
                shift_mine[k] = jnp.full(shift_mine.shape[1:], move_ref[0, k], jnp.int32)
                shift_of[0, k] = jnp.full(shift_mine.shape[1:], move_ref[0, k], jnp.int32)
                mine_key[k] = rounded(fresh_rows(k))

            @pl.when(column == hub)
            def _():
                pl.semaphore_wait(plane_sem, groups - 1)
                for e in range(1, columns):
                    pl.semaphore_signal(
                        open_sem, inc=1, device_id=at_column(e), device_id_type=MESH
                    )

        if c == cuts - 1:
            @pl.when(column != hub)
            def _():
                pl.semaphore_wait(open_sem, 1)

            for copy in mine_copies + newer_copies + shift_copies:
                launch(copy)

    absorb(settled, first, 0, between)
    for copy in key_copies:
        copy.start()
    wv_copy.start()
    for k in range(holders):
        newer[k] = jnp.zeros((EXTRA, entries), jnp.bfloat16)
        newer[k, 0:16] = rounded(fresh_rows(k))
    for copy in key_copies:
        copy.wait()

    at_key = lax.broadcasted_iota(jnp.int32, (1, total), 1)
    at_row = lax.broadcasted_iota(jnp.int32, (unit_rows, 1), 0)
    within = lax.rem(lax.div(at_row, cut), PAIR)
    turns_in = set()

    def attend(member):
        span, k = member
        u = number[member]
        late = int(member in moving)
        for e in range(1, columns):
            for c in range(lat_pieces(member)):
                lat_copy(member, e, c).wait_recv()
            if late not in turns_in:
                rot_copy(late, e).wait_recv()
        turns_in.add(late)
        live = length_ref[(rank * columns + column) * holders + k]
        token = jnp.where(at_key < capacity, steps, at_key - capacity)
        token = jnp.where(at_key < live, -1, token)
        nt = (((1,), (1,)), ((), ()))
        queries = lat_recv[u].reshape(unit_rows, latent)
        turns = jnp.concatenate(
            [
                rot_recv[e, u][c * cut : (c + 1) * cut, s * rope : (s + 1) * rope]
                for e in range(columns)
                for c in range(cuts)
                for s in range(PAIR)
            ],
            axis=0,
        )
        cached = jnp.dot(
            queries, keys[k, :latent], preferred_element_type=jnp.float32
        ) + jnp.dot(turns, keys[k, latent:], preferred_element_type=jnp.float32)
        decoded = lax.dot_general(
            queries, newer[k, :, :latent], nt, preferred_element_type=jnp.float32
        ) + lax.dot_general(
            turns, newer[k, :, latent:], nt, preferred_element_type=jnp.float32
        )
        scores = jnp.concatenate([cached, decoded], axis=1)
        scores = jnp.where(token <= span * PAIR + within, scores * scale, -jnp.inf)
        spread = jnp.exp(scores - jnp.max(scores, axis=1, keepdims=True))
        weights = rounded(spread / jnp.sum(spread, axis=1, keepdims=True))
        mixed = rounded(
            lax.dot_general(
                weights[:, :capacity], keys[k, :latent], nt, preferred_element_type=jnp.float32
            )
            + jnp.dot(
                weights[:, capacity:], newer[k, :, :latent], preferred_element_type=jnp.float32
            )
        ).reshape(columns, PAIR * heads, latent)
        back_recv[u, 0] = mixed[0]
        for e in range(1, columns):
            back_send[u, e] = mixed[e]

    def give_back(members):
        for member in members:
            for c in range(back_pieces(member)):
                for e in downward:
                    launch(back_copy(member, e, c))

    def project(member, c):
        span, k = member
        u = number[member]
        chunks = range(cuts) if c is None else [c]
        for e in range(1, columns):
            for j in range(back_pieces(member)) if c is None else [c]:
                back_copy(member, e, j).wait_recv()
        for e in range(columns):
            for j in chunks:
                for s in range(PAIR):
                    at = (j * PAIR + s) * cut
                    value = wide(back_recv[u, e, at : at + cut])
                    for l in range(latent // LANES):
                        rows_mid[l, pl.ds(place(0, e, s) + j * cut, cut)] = value[:, lane(l)]

        def head(i, carry):
            at = pl.ds(i, columns * PAIR, stride=heads)
            picked = jnp.concatenate(
                [rounded(rows_mid[l, at]) for l in range(latent // LANES)], axis=1
            )
            rows_out[at] = jnp.dot(picked, wv[i], preferred_element_type=jnp.float32)
            return carry

        count = len(chunks) * cut
        start = chunks[0] * cut
        lax.fori_loop(start, start + count, head, 0, unroll=min(count, 8))
        for e in range(columns):
            for s in range(PAIR):
                value = rounded(rows_out[pl.ds(place(0, e, s) + start, count)])
                if member in moving:
                    home[k, s, e, start : start + count] = value
                else:
                    out_ref[span * PAIR + s, slot(e, k), start : start + count] = value

    attend(first[0])
    give_back(first[:1])
    for copy in mine_copies + newer_copies + shift_copies:
        copy.wait_recv()
    turn(moving, 1)
    for e in upward:
        launch(rot_copy(1, e))
    absorb(moving, moving, 1, lambda c: None)
    for member in rest:
        for e in upward:
            launch(lat_copy(member, e, 0))
    for member in first[1:]:
        attend(member)
    for k in range(movers):
        later = chosen(0, k, lambda n: moved_key[n, k])
        newer[k, 0:16] = rounded(jnp.where(row < PAIR, wide(newer[k, 0:16]), later))
    for member in moving:
        attend(member)
    give_back(moving + first[1:])
    wv_copy.wait()
    project(first[0], None)
    for member in rest:
        attend(member)
    give_back(rest)
    for member in moving:
        project(member, None)
    for copy in home_copies:
        launch(copy)
    for member in first[1:]:
        project(member, None)
    for copy in home_copies:
        copy.wait_recv()
    for k in range(movers):
        for e in range(columns):
            for s in range(PAIR):
                out_ref[PAIR + s, slot(e, k)] = rounded(
                    chosen(e, k, lambda n: home_recv[n, k, s, e])
                )
    for c in range(cuts):
        for member in rest:
            project(member, c)
    for copy in sent:
        copy.wait_send()


def local_part(heads):
    return max(heads // 4, 1)


def body(q_nope, q_rope, w_absorb_k, w_absorb_v, latent_cache, new_latent, lengths, moves):
    steps, slots, heads, width = q_nope.shape
    rope = q_rope.shape[3]
    latent = w_absorb_k.shape[2]
    holders, capacity, entries = latent_cache.shape
    movers = moves.shape[1]
    groups = lax.axis_size("grp")
    columns = lax.axis_size("head")
    scale = YARN_GAIN / math.sqrt(width + rope)
    assert steps == 2 * PAIR
    units = steps // PAIR * holders
    rows = (2 * holders - movers) * columns * PAIR * heads
    others = groups - 1
    bf16, f32 = jnp.bfloat16, jnp.float32
    dma = pltpu.SemaphoreType.DMA
    hbm = pl.BlockSpec(memory_space=pl.ANY)
    parts = heads // local_part(heads)
    cuts = 1 if heads % 32 else 2
    here = functools.partial(pltpu.with_memory_space_constraint, memory_space=pltpu.HBM)
    arrays = (
        q_nope, q_rope, new_latent, w_absorb_k, w_absorb_v, jnp.swapaxes(latent_cache, 1, 2)
    )
    return pl.pallas_call(
        functools.partial(kernel, groups, columns, scale),
        out_shape=pltpu.VMEM(q_nope.shape, bf16),
        in_specs=[hbm, pl.BlockSpec(memory_space=pltpu.SMEM)] + [hbm] * len(arrays),
        out_specs=pl.BlockSpec(memory_space=pltpu.VMEM),
        scratch_shapes=[
            pltpu.SMEM(lengths.shape, jnp.int32),
            pltpu.VMEM(q_nope.shape, bf16),
            pltpu.VMEM(q_rope.shape, bf16),
            pltpu.VMEM(new_latent.shape, bf16),
            dma((4,)),
            pltpu.VMEM(w_absorb_k.shape, bf16),
            pltpu.VMEM(w_absorb_v.shape, bf16),
            pltpu.VMEM((holders, entries, capacity), bf16),
            pltpu.VMEM((holders, EXTRA, entries), bf16),
            dma((parts + holders + 1,)),
            pltpu.VMEM((rows, width), f32),
            pltpu.VMEM((latent // LANES, rows, LANES), f32),
            pltpu.VMEM((rows, width), f32),
            pltpu.VMEM((units, columns, PAIR * heads, latent), bf16),
            pltpu.VMEM((units, columns, PAIR * heads, latent), bf16),
            pltpu.VMEM((columns, units, heads, PAIR * rope), bf16),
            pltpu.VMEM((columns, units, heads, PAIR * rope), bf16),
            pltpu.VMEM((units, columns, PAIR * heads, latent), bf16),
            pltpu.VMEM((units, columns, PAIR * heads, latent), bf16),
            pltpu.VMEM((movers, PAIR + 1, columns, heads, width), bf16),
            pltpu.VMEM((others, movers, PAIR + 1, columns, heads, width), bf16),
            pltpu.VMEM((movers, 16, entries), bf16),
            pltpu.VMEM((others, movers, 16, entries), bf16),
            pltpu.VMEM((movers, PAIR, columns, heads, width), bf16),
            pltpu.VMEM((others, movers, PAIR, columns, heads, width), bf16),
            pltpu.VMEM((columns, movers, 8, LANES), jnp.int32),
            pltpu.VMEM((movers, 8, LANES), jnp.int32),
            dma((units, columns, cuts)), dma((units, columns, cuts)),
            dma((2, columns)), dma((2, columns)),
            dma((units, columns, cuts)), dma((units, columns, cuts)),
            dma((others,)), dma((others,)),
            dma((others,)), dma((others,)),
            dma((others,)), dma((others,)),
            dma((columns,)), dma((columns,)),
            pltpu.SemaphoreType.REGULAR, pltpu.SemaphoreType.REGULAR,
        ],
        compiler_params=pltpu.CompilerParams(
            collective_id=0, has_side_effects=True, vmem_limit_bytes=44 << 20
        ),
    )(here(lengths), moves, *map(here, arrays))


def solution(mesh):
    placed = (
        P(None, "grp", "head", None),
        P(None, "grp", "head", None),
        P("head", None, None),
        P("head", None, None),
        P(("grp", "head"), None, None),
        P(None, ("grp", "head"), None),
        P(),
        P("head", None),
    )
    return jax.shard_map(
        body, mesh=mesh, in_specs=placed, out_specs=P(None, "grp", "head", None), check_vma=False
    )
```

```python
import functools
import math

import jax
import jax.numpy as jnp
from jax import lax
from jax.experimental import pallas as pl
from jax.experimental.pallas import tpu as pltpu
from jax.sharding import PartitionSpec as P

PAIR = 2
EXTRA = 128
LANES = 128
YARN_GAIN = (0.1 * math.log(40.0) + 1.0) ** 2
MESH = pl.DeviceIdType.MESH


def lane(c):
    return slice(c * LANES, (c + 1) * LANES)


def rounded(value):
    return value.astype(jnp.bfloat16)


def wide(value):
    return value.astype(jnp.float32)


def kernel(
    groups, columns, scale,
    length_hbm, move_ref, nope_hbm, rope_hbm, fresh_hbm, wk_hbm, wv_hbm, cache_hbm,
    out_ref,
    length_ref, nope_ref, rope_ref, fresh_ref, entry_sem,
    wk, wv, keys, newer, local_sem,
    rows_in, rows_mid, rows_out,
    lat_send, lat_recv, rot_send, rot_recv, back_send, back_recv,
    mine, moved, mine_key, moved_key, home, home_recv, shift_of, shift_mine,
    lat_ss, lat_rs, rot_ss, rot_rs, back_ss, back_rs,
    mine_ss, mine_rs, key_ss, key_rs, home_ss, home_rs, shift_ss, shift_rs,
    near_sem, rank_sem, plane_sem, open_sem,
):
    steps, _, heads, _ = nope_ref.shape
    holders, entries, capacity = cache_hbm.shape
    latent = wk.shape[2]
    rope = entries - latent
    movers = move_ref.shape[1]
    total = capacity + EXTRA
    cuts = cuts_of(heads)
    cut = heads // cuts
    rank = lax.axis_index("grp")
    column = lax.axis_index("head")
    parts = wk.shape[0] // local_part(heads)
    part = local_part(heads)

    first = [(0, k) for k in range(holders)]
    rest = [(1, k) for k in range(movers, holders)]
    moving = [(1, k) for k in range(movers)]
    settled = first + rest
    number = {member: u for u, member in enumerate(settled + moving)}

    def at_column(e):
        return (rank, lax.rem(column + e + columns, columns))

    def at_group(d):
        return (lax.rem(rank + d + groups, groups), column)

    barrier = pltpu.get_barrier_semaphore()
    for e in range(1, columns):
        @pl.when(column + e < columns)
        def _():
            pl.semaphore_signal(barrier, inc=1, device_id=at_column(e), device_id_type=MESH)

    for d in range(1, groups):
        @pl.when(jnp.logical_and(column == 0, rank + d < groups))
        def _():
            pl.semaphore_signal(barrier, inc=1, device_id=at_group(d), device_id_type=MESH)

    wk_copies = [
        pltpu.make_async_copy(
            wk_hbm.at[pl.ds(n * part, part)], wk.at[pl.ds(n * part, part)], local_sem.at[n]
        )
        for n in range(parts)
    ]
    key_copy = pltpu.make_async_copy(cache_hbm, keys, local_sem.at[parts])
    wv_copy = pltpu.make_async_copy(wv_hbm, wv, local_sem.at[parts + 1])
    entry_copies = [
        pltpu.make_async_copy(src, dst, entry_sem.at[n])
        for n, (src, dst) in enumerate(
            (
                (rope_hbm, rope_ref), (nope_hbm, nope_ref), (fresh_hbm, fresh_ref),
                (length_hbm, length_ref),
            )
        )
    ]
    for copy in entry_copies[:2] + wk_copies + entry_copies[2:]:
        copy.start()

    below = jnp.where(column == 0, rank, column)

    @pl.when(below > 0)
    def _():
        pl.semaphore_wait(barrier, below)

    for e in range(1, columns):
        @pl.when(column >= e)
        def _():
            pl.semaphore_signal(
                near_sem.at[e - 1], inc=1, device_id=at_column(-e), device_id_type=MESH
            )

    for d in range(1, groups):
        @pl.when(jnp.logical_and(column == 0, rank >= d))
        def _():
            pl.semaphore_signal(
                rank_sem, inc=1, device_id=at_group(-d), device_id_type=MESH
            )

    def remote(src, dst, send, recv, target):
        return pltpu.make_async_remote_copy(
            src_ref=src, dst_ref=dst, send_sem=send, recv_sem=recv,
            device_id=target, device_id_type=MESH,
        )

    def slot(e, k):
        return lax.rem(column + e, columns) * holders + k

    def turned(span, e, k):
        return jnp.concatenate(
            [rope_ref[span * PAIR + s, slot(e, k)] for s in range(PAIR)], axis=1
        )

    def shift_copy(e):
        return remote(shift_mine, shift_of.at[columns - e], shift_ss, shift_rs, at_column(e))

    def mine_copy(d):
        return remote(mine, moved.at[d - 1], mine_ss, mine_rs, at_group(-d))

    def newer_copy(d):
        return remote(mine_key, moved_key.at[d - 1], key_ss, key_rs, at_group(-d))

    def home_copy(d):
        return remote(home, home_recv.at[d - 1], home_ss, home_rs, at_group(d))

    per = PAIR * cut
    others = pl.ds(1, columns - 1)
    def lat_copy(member, e, c):
        u = number[member]
        at = pl.ds(c * per, per) if member == first[0] else pl.ds(0, PAIR * heads)
        return remote(
            lat_send.at[u, e, at], lat_recv.at[u, e, at], lat_ss, lat_rs.at[u], at_column(e)
        )

    def lat_all(member):
        u = number[member]
        return remote(
            lat_send.at[u, others], lat_recv.at[u, others], lat_ss, lat_rs.at[u], at_column(1)
        )

    def rot_copy(late, e):
        at = pl.ds(len(settled), len(moving)) if late else pl.ds(0, len(settled))
        return remote(
            rot_send.at[e, at], rot_recv.at[e, at], rot_ss, rot_rs.at[late], at_column(e)
        )

    def back_pieces(member):
        return cuts if member in rest else 1

    landed = {}
    for member in settled + moving:
        for c in range(back_pieces(member)):
            landed[member, c] = len(landed)

    def back_copy(member, e, c):
        u = number[member]
        at = pl.ds(c * per, per) if member in rest else pl.ds(0, PAIR * heads)
        return remote(
            back_send.at[u, e, at], back_recv.at[u, e, at], back_ss,
            back_rs.at[landed[member, c]], at_column(-e),
        )

    def back_all(member, c):
        u = number[member]
        at = pl.ds(c * per, per) if member in rest else pl.ds(0, PAIR * heads)
        return remote(
            back_send.at[u, others, at], back_recv.at[u, others, at], back_ss,
            back_rs.at[landed[member, c]], at_column(1),
        )

    low, high = jnp.int32(0), jnp.int32(columns - 1)
    upward, downward = [], []
    for _ in range(columns - 1):
        take_high = high - column >= column - low
        target = jnp.where(take_high, high, low)
        upward.append(lax.rem(target - column + columns, columns))
        downward.append(lax.rem(column - target + columns, columns))
        high = jnp.where(take_high, high - 1, high)
        low = jnp.where(take_high, low, low + 1)

    odd = lax.rem(rank, 2) == 1

    def staggered(order):
        turned_by_one = order[-1:] + order[:-1]
        return [jnp.where(odd, b, a) for a, b in zip(order, turned_by_one)]

    order_a = order_b = staggered(upward)
    order_c = order_d = order_e = staggered(downward)

    def chosen(e, k, options):
        found = wide(options(0))
        for d in range(2, groups):
            is_it = shift_of[e, k, 0:1, 0:1] == d
            found = jnp.where(is_it, wide(options(d - 1)), found)
        return found

    unit_rows = columns * PAIR * heads

    def place(m, e, s):
        return ((m * columns + e) * PAIR + s) * heads

    def turn(members, late):
        for span, k in members:
            u = number[span, k]
            for e in range(columns):
                if late:
                    pair = rounded(chosen(e, k, lambda n: moved[n, k, PAIR, e]))
                else:
                    pair = turned(span, e, k)
                if e:
                    rot_send[e, u] = pair
                else:
                    rot_recv[0, u] = pair

    def absorb(members, late, after):
        count = len(members) * columns * PAIR
        for m, (span, k) in enumerate(members):
            for e in range(columns):
                for s in range(PAIR):
                    if late:
                        value = chosen(e, k, lambda n: moved[n, k, s, e])
                    else:
                        value = wide(nope_ref[span * PAIR + s, slot(e, k)])
                    rows_in[pl.ds(place(m, e, s), heads)] = value
        for n in range(parts):
            if not late:
                wk_copies[n].wait()

            def head(i, carry):
                picked = rounded(rows_in[pl.ds(i, count, stride=heads)])
                result = jnp.dot(picked, wk[i], preferred_element_type=jnp.float32)
                for c in range(latent // LANES):
                    rows_mid[c, pl.ds(i, count, stride=heads)] = result[:, lane(c)]
                return carry

            lax.fori_loop(n * part, (n + 1) * part, head, 0, unroll=True)
            if (n + 1) % (parts // cuts):
                continue
            c = n // (parts // cuts)
            for m, member in enumerate(members):
                u = number[member]
                for e in range(columns):
                    value = jnp.concatenate(
                        [
                            jnp.concatenate(
                                [
                                    rounded(rows_mid[l, pl.ds(place(m, e, s) + c * cut, cut)])
                                    for l in range(latent // LANES)
                                ],
                                axis=1,
                            )
                            for s in range(PAIR)
                        ],
                        axis=0,
                    )
                    if e:
                        lat_send[u, e, c * per : (c + 1) * per] = value
                    else:
                        lat_recv[u, 0, c * per : (c + 1) * per] = value
            after(c)

    entry_copies[0].wait()
    turn(settled, 0)
    for k in range(movers):
        shift_mine[k] = jnp.full(shift_mine.shape[1:], move_ref[0, k], jnp.int32)
        shift_of[0, k] = jnp.full(shift_mine.shape[1:], move_ref[0, k], jnp.int32)
    for e in range(1, columns):
        @pl.when(column + e >= columns)
        def _():
            rot_copy(0, e).start()
            shift_copy(e).start()

    for copy in entry_copies[1:]:
        copy.wait()
    row = lax.broadcasted_iota(jnp.int32, (16, entries), 0)

    def fresh_rows(k):
        found = jnp.zeros((16, entries), jnp.float32)
        for j in range(steps):
            found = jnp.where(row == j, wide(fresh_ref[j])[k : k + 1], found)
        return found

    def after_settled(c):
        if c == 0:
            for e in range(1, columns):
                @pl.when(column + e < columns)
                def _():
                    pl.semaphore_wait(near_sem.at[e - 1], 1)
                    rot_copy(0, e).start()
                    shift_copy(e).start()

                lat_copy(first[0], e, 0).start()

            @pl.when(jnp.logical_and(column == 0, rank < groups - 1))
            def _():
                pl.semaphore_wait(rank_sem, groups - 1 - rank)

            @pl.when(column == 0)
            def _():
                for d in range(1, groups):
                    pl.semaphore_signal(
                        plane_sem, inc=1, device_id=at_group(d), device_id_type=MESH
                    )

            for k in range(movers):
                for e in range(columns):
                    for s in range(PAIR):
                        mine[k, s, e] = nope_ref[PAIR + s, slot(e, k)]
                    mine[k, PAIR, e] = turned(1, e, k)
                mine_key[k] = rounded(fresh_rows(k))

        if c == cuts - 1:
            if cuts > 1:
                for e in order_a:
                    lat_copy(first[0], e, c).start()
            for member in first[1:]:
                for e in order_a:
                    lat_copy(member, e, 0).start()

            @pl.when(column == 0)
            def _():
                pl.semaphore_wait(plane_sem, groups - 1)
                for e in range(1, columns):
                    pl.semaphore_signal(
                        open_sem, inc=1, device_id=at_column(e), device_id_type=MESH
                    )

            @pl.when(column > 0)
            def _():
                pl.semaphore_wait(open_sem, 1)

            for d in range(1, groups):
                mine_copy(d).start()
            for d in range(1, groups):
                newer_copy(d).start()
            for member in rest:
                for e in order_b:
                    lat_copy(member, e, 0).start()

    absorb(settled, 0, after_settled)
    key_copy.start()
    wv_copy.start()
    for k in range(holders):
        newer[k] = jnp.zeros((EXTRA, entries), jnp.bfloat16)
        newer[k, 0:16] = rounded(fresh_rows(k))
    key_copy.wait()

    at_key = lax.broadcasted_iota(jnp.int32, (1, total), 1)
    at_row = lax.broadcasted_iota(jnp.int32, (unit_rows, 1), 0)
    within = lax.rem(lax.div(at_row, cut), PAIR)
    turns_in = set()

    def attend(member):
        span, k = member
        u = number[member]
        late = int(member in moving)
        lat_all(member).wait_recv()
        if late not in turns_in:
            at = pl.ds(len(settled), len(moving)) if late else pl.ds(0, len(settled))
            remote(
                rot_send.at[others, at], rot_recv.at[others, at], rot_ss, rot_rs.at[late],
                at_column(1),
            ).wait_recv()
        turns_in.add(late)
        live = length_ref[(rank * columns + column) * holders + k]
        token = jnp.where(at_key < capacity, steps, at_key - capacity)
        token = jnp.where(at_key < live, -1, token)
        nt = (((1,), (1,)), ((), ()))
        queries = lat_recv[u].reshape(unit_rows, latent)
        turns = jnp.concatenate(
            [
                rot_recv[e, u][c * cut : (c + 1) * cut, s * rope : (s + 1) * rope]
                for e in range(columns)
                for c in range(cuts)
                for s in range(PAIR)
            ],
            axis=0,
        )
        cached = jnp.dot(
            queries, keys[k, :latent], preferred_element_type=jnp.float32
        ) + jnp.dot(turns, keys[k, latent:], preferred_element_type=jnp.float32)
        decoded = lax.dot_general(
            queries, newer[k, :, :latent], nt, preferred_element_type=jnp.float32
        ) + lax.dot_general(
            turns, newer[k, :, latent:], nt, preferred_element_type=jnp.float32
        )
        scores = jnp.concatenate([cached, decoded], axis=1)
        scores = jnp.where(token <= span * PAIR + within, scores * scale, -jnp.inf)
        spread = jnp.exp(scores - jnp.max(scores, axis=1, keepdims=True))
        weights = rounded(spread / jnp.sum(spread, axis=1, keepdims=True))
        mixed = rounded(
            lax.dot_general(
                weights[:, :capacity], keys[k, :latent], nt, preferred_element_type=jnp.float32
            )
            + jnp.dot(
                weights[:, capacity:], newer[k, :, :latent], preferred_element_type=jnp.float32
            )
        ).reshape(columns, PAIR * heads, latent)
        back_recv[u, 0] = mixed[0]
        for e in range(1, columns):
            back_send[u, e] = mixed[e]

    def give_back(members, order):
        for member in members:
            for c in range(back_pieces(member)):
                for e in order:
                    back_copy(member, e, c).start()

    def project(member, c):
        span, k = member
        u = number[member]
        chunks = range(cuts) if c is None else [c]
        for j in range(back_pieces(member)) if c is None else [c]:
            back_all(member, j).wait_recv()
        for e in range(columns):
            for j in chunks:
                for s in range(PAIR):
                    at = (j * PAIR + s) * cut
                    value = wide(back_recv[u, e, at : at + cut])
                    for l in range(latent // LANES):
                        rows_mid[l, pl.ds(place(0, e, s) + j * cut, cut)] = value[:, lane(l)]

        def head(i, carry):
            at = pl.ds(i, columns * PAIR, stride=heads)
            picked = jnp.concatenate(
                [rounded(rows_mid[l, at]) for l in range(latent // LANES)], axis=1
            )
            rows_out[at] = jnp.dot(picked, wv[i], preferred_element_type=jnp.float32)
            return carry

        count = len(chunks) * cut
        start = chunks[0] * cut
        lax.fori_loop(start, start + count, head, 0, unroll=min(count, 8))
        for e in range(columns):
            for s in range(PAIR):
                value = rounded(rows_out[pl.ds(place(0, e, s) + start, count)])
                if member in moving:
                    home[k, s, e, start : start + count] = value
                else:
                    out_ref[span * PAIR + s, slot(e, k), start : start + count] = value

    attend(first[0])
    shifts = remote(shift_of.at[others], shift_of.at[others], shift_ss, shift_rs, at_column(1))
    mines = remote(moved, moved, mine_ss, mine_rs, at_group(1))
    newers = remote(moved_key, moved_key, key_ss, key_rs, at_group(1))
    homes = remote(home_recv, home_recv, home_ss, home_rs, at_group(1))
    for copy in (shifts, mines, newers):
        copy.wait_recv()
    turn(moving, 1)
    for e in order_b:
        rot_copy(1, e).start()
    absorb(moving, 1, lambda c: None)
    for member in moving:
        for e in order_b:
            lat_copy(member, e, 0).start()
    give_back(first[:1], order_c)
    for member in first[1:] + rest:
        attend(member)
    for k in range(movers):
        later = chosen(0, k, lambda n: moved_key[n, k])
        newer[k, 0:16] = rounded(jnp.where(row < PAIR, wide(newer[k, 0:16]), later))
    for member in moving:
        attend(member)
    give_back(moving + first[1:], order_d)
    give_back(rest, order_e)
    wv_copy.wait()
    project(first[0], None)
    for member in moving:
        project(member, None)
    for d in range(1, groups):
        home_copy(d).start()
    for member in first[1:]:
        project(member, None)
    homes.wait_recv()
    for k in range(movers):
        for e in range(columns):
            for s in range(PAIR):
                out_ref[PAIR + s, slot(e, k)] = rounded(
                    chosen(e, k, lambda n: home_recv[n, k, s, e])
                )
    for c in range(cuts):
        for member in rest:
            project(member, c)
    every = remote(lat_send.at[:, others], lat_recv.at[:, others], lat_ss, lat_rs.at[0], at_column(1))
    every.wait_send()
    remote(
        rot_send.at[others], rot_recv.at[others], rot_ss, rot_rs.at[0], at_column(1)
    ).wait_send()
    remote(
        back_send.at[:, others], back_recv.at[:, others], back_ss, back_rs.at[0], at_column(1)
    ).wait_send()
    for copy in (shifts, mines, newers, homes):
        copy.wait_send()


def local_part(heads):
    return max(heads // 4, 1)


def cuts_of(heads):
    return 1 if heads % 32 else 2


def body(q_nope, q_rope, w_absorb_k, w_absorb_v, latent_cache, new_latent, lengths, moves):
    steps, slots, heads, width = q_nope.shape
    rope = q_rope.shape[3]
    latent = w_absorb_k.shape[2]
    holders, capacity, entries = latent_cache.shape
    movers = moves.shape[1]
    groups = lax.axis_size("grp")
    columns = lax.axis_size("head")
    scale = YARN_GAIN / math.sqrt(width + rope)
    assert steps == 2 * PAIR
    units = steps // PAIR * holders
    rows = (2 * holders - movers) * columns * PAIR * heads
    others = groups - 1
    bf16, f32 = jnp.bfloat16, jnp.float32
    dma = pltpu.SemaphoreType.DMA
    hbm = pl.BlockSpec(memory_space=pl.ANY)
    parts = heads // local_part(heads)
    cuts = cuts_of(heads)
    here = functools.partial(pltpu.with_memory_space_constraint, memory_space=pltpu.HBM)
    arrays = (
        q_nope, q_rope, new_latent, w_absorb_k, w_absorb_v, jnp.swapaxes(latent_cache, 1, 2)
    )
    return pl.pallas_call(
        functools.partial(kernel, groups, columns, scale),
        out_shape=pltpu.VMEM(q_nope.shape, bf16),
        in_specs=[hbm, pl.BlockSpec(memory_space=pltpu.SMEM)] + [hbm] * len(arrays),
        out_specs=pl.BlockSpec(memory_space=pltpu.VMEM),
        scratch_shapes=[
            pltpu.SMEM(lengths.shape, jnp.int32),
            pltpu.VMEM(q_nope.shape, bf16),
            pltpu.VMEM(q_rope.shape, bf16),
            pltpu.VMEM(new_latent.shape, bf16),
            dma((4,)),
            pltpu.VMEM(w_absorb_k.shape, bf16),
            pltpu.VMEM(w_absorb_v.shape, bf16),
            pltpu.VMEM((holders, entries, capacity), bf16),
            pltpu.VMEM((holders, EXTRA, entries), bf16),
            dma((parts + 2,)),
            pltpu.VMEM((rows, width), f32),
            pltpu.VMEM((latent // LANES, rows, LANES), f32),
            pltpu.VMEM((rows, width), f32),
            pltpu.VMEM((units, columns, PAIR * heads, latent), bf16),
            pltpu.VMEM((units, columns, PAIR * heads, latent), bf16),
            pltpu.VMEM((columns, units, heads, PAIR * rope), bf16),
            pltpu.VMEM((columns, units, heads, PAIR * rope), bf16),
            pltpu.VMEM((units, columns, PAIR * heads, latent), bf16),
            pltpu.VMEM((units, columns, PAIR * heads, latent), bf16),
            pltpu.VMEM((movers, PAIR + 1, columns, heads, width), bf16),
            pltpu.VMEM((others, movers, PAIR + 1, columns, heads, width), bf16),
            pltpu.VMEM((movers, 16, entries), bf16),
            pltpu.VMEM((others, movers, 16, entries), bf16),
            pltpu.VMEM((movers, PAIR, columns, heads, width), bf16),
            pltpu.VMEM((others, movers, PAIR, columns, heads, width), bf16),
            pltpu.VMEM((columns, movers, 8, LANES), jnp.int32),
            pltpu.VMEM((movers, 8, LANES), jnp.int32),
            dma, dma((units,)),
            dma, dma((2,)),
            dma, dma((units + (cuts - 1) * (holders - movers),)),
            dma, dma, dma, dma, dma, dma, dma, dma,
            pltpu.SemaphoreType.REGULAR((columns - 1,)), pltpu.SemaphoreType.REGULAR,
            pltpu.SemaphoreType.REGULAR, pltpu.SemaphoreType.REGULAR,
        ],
        compiler_params=pltpu.CompilerParams(
            collective_id=0, has_side_effects=True, vmem_limit_bytes=44 << 20
        ),
    )(here(lengths), moves, *map(here, arrays))


def solution(mesh):
    placed = (
        P(None, "grp", "head", None),
        P(None, "grp", "head", None),
        P("head", None, None),
        P("head", None, None),
        P(("grp", "head"), None, None),
        P(None, ("grp", "head"), None),
        P(),
        P("head", None),
    )
    return jax.shard_map(
        body, mesh=mesh, in_specs=placed, out_specs=P(None, "grp", "head", None), check_vma=False
    )
```

```python
import functools
import math

import jax
import jax.numpy as jnp
from jax import lax
from jax.experimental import pallas as pl
from jax.experimental.pallas import tpu as pltpu
from jax.sharding import PartitionSpec as P

PAIR = 2
EXTRA = 128
LANES = 128
YARN_GAIN = (0.1 * math.log(40.0) + 1.0) ** 2
MESH = pl.DeviceIdType.MESH


def lane(c):
    return slice(c * LANES, (c + 1) * LANES)


def rounded(value):
    return value.astype(jnp.bfloat16)


def wide(value):
    return value.astype(jnp.float32)


def kernel(
    groups, columns, scale,
    length_hbm, move_ref, nope_hbm, rope_hbm, fresh_hbm, wk_hbm, wv_hbm, cache_hbm,
    out_ref,
    length_ref, nope_ref, rope_ref, fresh_ref, entry_sem,
    wk, wv, keys, newer, local_sem,
    rows_in, rows_mid, rows_out,
    lat_send, lat_recv, late_send, late_recv, rot_send, rot_recv, back_send, back_recv,
    mine, moved, mine_key, moved_key, home, home_recv, shift_of, shift_mine,
    lat_ss, lat_rs, late_ss, late_rs, rot_ss, rot_rs, back_ss, back_rs,
    mine_ss, mine_rs, key_ss, key_rs, home_ss, home_rs, shift_ss, shift_rs,
    near_sem, rank_sem,
):
    steps, _, heads, _ = nope_ref.shape
    holders, entries, capacity = cache_hbm.shape
    latent = wk.shape[2]
    rope = entries - latent
    movers = move_ref.shape[1]
    total = capacity + EXTRA
    cuts = cuts_of(heads)
    cut = heads // cuts
    rank = lax.axis_index("grp")
    column = lax.axis_index("head")
    parts = wk.shape[0] // local_part(heads)
    part = local_part(heads)

    first = [(0, k) for k in range(holders)]
    rest = [(1, k) for k in range(movers, holders)]
    moving = [(1, k) for k in range(movers)]
    settled = first + rest
    number = {member: u for u, member in enumerate(settled + moving)}

    def at_column(e):
        return (rank, lax.rem(column + e + columns, columns))

    def at_group(d):
        return (lax.rem(rank + d + groups, groups), column)

    barrier = pltpu.get_barrier_semaphore()
    for e in range(1, columns):
        @pl.when(column + e < columns)
        def _():
            pl.semaphore_signal(barrier, inc=1, device_id=at_column(e), device_id_type=MESH)

    for d in range(1, groups):
        @pl.when(rank + d < groups)
        def _():
            pl.semaphore_signal(barrier, inc=1, device_id=at_group(d), device_id_type=MESH)

    wk_copies = [
        pltpu.make_async_copy(
            wk_hbm.at[pl.ds(n * part, part)], wk.at[pl.ds(n * part, part)], local_sem.at[n]
        )
        for n in range(parts)
    ]
    key_copy = pltpu.make_async_copy(cache_hbm, keys, local_sem.at[parts])
    wv_copy = pltpu.make_async_copy(wv_hbm, wv, local_sem.at[parts + 1])
    entry_copies = [
        pltpu.make_async_copy(src, dst, entry_sem.at[n])
        for n, (src, dst) in enumerate(
            (
                (rope_hbm, rope_ref), (nope_hbm, nope_ref), (fresh_hbm, fresh_ref),
                (length_hbm, length_ref),
            )
        )
    ]
    for copy in entry_copies[:2] + wk_copies[:1]:
        copy.start()

    below = rank + column

    @pl.when(below > 0)
    def _():
        pl.semaphore_wait(barrier, below)

    for e in range(1, columns):
        @pl.when(column >= e)
        def _():
            pl.semaphore_signal(
                near_sem.at[e - 1], inc=1, device_id=at_column(-e), device_id_type=MESH
            )

    for d in range(1, groups):
        @pl.when(rank >= d)
        def _():
            pl.semaphore_signal(
                rank_sem, inc=1, device_id=at_group(-d), device_id_type=MESH
            )

    def remote(src, dst, send, recv, target):
        return pltpu.make_async_remote_copy(
            src_ref=src, dst_ref=dst, send_sem=send, recv_sem=recv,
            device_id=target, device_id_type=MESH,
        )

    def slot(e, k):
        return lax.rem(column + e, columns) * holders + k

    def turned(span, e, k):
        return jnp.concatenate(
            [rope_ref[span * PAIR + s, slot(e, k)] for s in range(PAIR)], axis=1
        )

    def shift_copy(e):
        return remote(shift_mine, shift_of.at[columns - e], shift_ss, shift_rs, at_column(e))

    def mine_copy(d):
        return remote(mine, moved.at[d - 1], mine_ss, mine_rs, at_group(-d))

    def newer_copy(d):
        return remote(mine_key, moved_key.at[d - 1], key_ss, key_rs, at_group(-d))

    def home_copy(d):
        return remote(home, home_recv.at[d - 1], home_ss, home_rs, at_group(d))

    per = PAIR * cut
    others = pl.ds(1, columns - 1)
    halves = [(0, cuts // 2), (cuts // 2, cuts)] if cuts > 1 else [(0, 1)]
    back_pieces = {member: [(0, cuts)] for member in number}
    if cuts > 1:
        for member in rest:
            back_pieces[member] = halves

    def rows_of(piece):
        return pl.ds(piece[0] * per, (piece[1] - piece[0]) * per)

    def lat_copy(e, c):
        return remote(lat_send.at[e, c], lat_recv.at[e, c], lat_ss, lat_rs, at_column(e))

    def late_copy(e):
        return remote(late_send.at[e], late_recv.at[e], late_ss, late_rs, at_column(e))

    lats = remote(lat_send.at[others], lat_recv.at[others], lat_ss, lat_rs, at_column(1))
    lates = remote(late_send.at[others], late_recv.at[others], late_ss, late_rs, at_column(1))

    def rot_copy(late, e):
        at = pl.ds(len(settled), len(moving)) if late else pl.ds(0, len(settled))
        return remote(
            rot_send.at[e, at], rot_recv.at[e, at], rot_ss, rot_rs.at[late], at_column(e)
        )

    landed = {}
    for member in settled + moving:
        for c in range(len(back_pieces[member])):
            landed[member, c] = len(landed)

    def back_copy(member, e, c):
        u = number[member]
        at = rows_of(back_pieces[member][c])
        return remote(
            back_send.at[u, e, at], back_recv.at[u, e, at], back_ss,
            back_rs.at[landed[member, c]], at_column(-e),
        )

    def back_all(member, c):
        u = number[member]
        at = rows_of(back_pieces[member][c])
        return remote(
            back_send.at[u, others, at], back_recv.at[u, others, at], back_ss,
            back_rs.at[landed[member, c]], at_column(1),
        )

    low, high = jnp.int32(0), jnp.int32(columns - 1)
    near = []
    for _ in range(columns - 1):
        above, below = high - column, column - low
        take_high = jnp.where(2 * column < columns, above >= below, above > below)
        near.insert(0, jnp.where(take_high, high, low))
        high = jnp.where(take_high, high - 1, high)
        low = jnp.where(take_high, low, low + 1)
    near_up = [lax.rem(target - column + columns, columns) for target in near]
    near_down = [lax.rem(column - target + columns, columns) for target in near]

    far_down = near_down[::-1]
    end = jnp.logical_or(column == 0, column == columns - 1)

    def send_back(pieces, order):
        for member, c in pieces:
            for e in order:
                back_copy(member, e, c).start()

    def pieces_of(members, table):
        return [(member, c) for member in members for c in range(len(table[member]))]

    def chosen(e, k, options):
        found = wide(options(0))
        for d in range(2, groups):
            is_it = shift_of[e, k, 0:1, 0:1] == d
            found = jnp.where(is_it, wide(options(d - 1)), found)
        return found

    unit_rows = columns * PAIR * heads

    def place(m, e, s):
        return ((m * columns + e) * PAIR + s) * heads

    def turn(members, late):
        for span, k in members:
            u = number[span, k]
            for e in range(columns):
                if late:
                    pair = rounded(chosen(e, k, lambda n: moved[n, k, PAIR, e]))
                else:
                    pair = turned(span, e, k)
                if e:
                    rot_send[e, u] = pair
                else:
                    rot_recv[0, u] = pair

    def absorb(members, late, after):
        count = len(members) * columns * PAIR
        for m, (span, k) in enumerate(members):
            for e in range(columns):
                for s in range(PAIR):
                    if late:
                        value = chosen(e, k, lambda n: moved[n, k, s, e])
                    else:
                        value = wide(nope_ref[span * PAIR + s, slot(e, k)])
                    rows_in[pl.ds(place(m, e, s), heads)] = value
        for n in range(parts):
            if not late:
                wk_copies[n].wait()

            def head(i, carry):
                picked = rounded(rows_in[pl.ds(i, count, stride=heads)])
                result = jnp.dot(picked, wk[i], preferred_element_type=jnp.float32)
                for c in range(latent // LANES):
                    rows_mid[c, pl.ds(i, count, stride=heads)] = result[:, lane(c)]
                return carry

            lax.fori_loop(n * part, (n + 1) * part, head, 0, unroll=True)
            if (n + 1) % (parts // cuts):
                continue
            c = n // (parts // cuts)
            for m, member in enumerate(members):
                u = number[member]
                for e in range(columns):
                    value = rounded(
                        jnp.concatenate(
                            [
                                jnp.concatenate(
                                    [
                                        rows_mid[l, pl.ds(place(m, e, s) + c * cut, cut)]
                                        for l in range(latent // LANES)
                                    ],
                                    axis=1,
                                )
                                for s in range(PAIR)
                            ],
                            axis=0,
                        )
                    )
                    if late:
                        to, at = (late_send if e else late_recv), (e, m, c)
                    else:
                        to, at = (lat_send if e else lat_recv), (e, c, m)
                    to[at] = value
            after(c)

    entry_copies[0].wait()
    for copy in wk_copies[1:] + entry_copies[2:]:
        copy.start()
    turn(settled, 0)
    for k in range(movers):
        shift_mine[k] = jnp.full(shift_mine.shape[1:], move_ref[0, k], jnp.int32)
        shift_of[0, k] = jnp.full(shift_mine.shape[1:], move_ref[0, k], jnp.int32)
    for e in range(1, columns):
        @pl.when(column + e >= columns)
        def _():
            rot_copy(0, e).start()
            shift_copy(e).start()

    entry_copies[1].wait()
    row = lax.broadcasted_iota(jnp.int32, (16, entries), 0)

    def fresh_rows(k):
        found = jnp.zeros((16, entries), jnp.float32)
        for j in range(steps):
            found = jnp.where(row == j, wide(fresh_ref[j])[k : k + 1], found)
        return found

    def after_settled(c):
        asked = 0
        for e in range(1, columns):
            @pl.when(column + e >= columns)
            def _():
                lat_copy(e, c).start()

            if c == asked:
                @pl.when(column + e < columns)
                def _():
                    pl.semaphore_wait(near_sem.at[e - 1], 1)
                    rot_copy(0, e).start()
                    shift_copy(e).start()

        if c >= asked:
            for e in range(1, columns):
                @pl.when(column + e < columns)
                def _():
                    for j in range(c + 1) if c == asked else [c]:
                        lat_copy(e, j).start()

        if c == 0:
            for copy in entry_copies[2:]:
                copy.wait()
            for k in range(movers):
                for e in range(columns):
                    for s in range(PAIR):
                        mine[k, s, e] = nope_ref[PAIR + s, slot(e, k)]
                    mine[k, PAIR, e] = turned(1, e, k)
                mine_key[k] = rounded(fresh_rows(k))

        if c == cuts - 1:
            @pl.when(rank < groups - 1)
            def _():
                pl.semaphore_wait(rank_sem, groups - 1 - rank)

            for d in range(1, groups):
                mine_copy(d).start()
            for d in range(1, groups):
                newer_copy(d).start()

    absorb(settled, 0, after_settled)
    key_copy.start()
    wv_copy.start()
    for k in range(holders):
        newer[k] = jnp.zeros((EXTRA, entries), jnp.bfloat16)
        newer[k, 0:16] = rounded(fresh_rows(k))
    key_copy.wait()

    at_key = lax.broadcasted_iota(jnp.int32, (1, total), 1)
    at_row = lax.broadcasted_iota(jnp.int32, (unit_rows, 1), 0)
    within = lax.rem(lax.div(at_row, cut), PAIR)
    turns_in = set()

    def attend(member):
        span, k = member
        u = number[member]
        late = int(member in moving)
        if late not in turns_in:
            (lates if late else lats).wait_recv()
        if late not in turns_in:
            at = pl.ds(len(settled), len(moving)) if late else pl.ds(0, len(settled))
            remote(
                rot_send.at[others, at], rot_recv.at[others, at], rot_ss, rot_rs.at[late],
                at_column(1),
            ).wait_recv()
        turns_in.add(late)
        live = length_ref[(rank * columns + column) * holders + k]
        token = jnp.where(at_key < capacity, steps, at_key - capacity)
        token = jnp.where(at_key < live, -1, token)
        nt = (((1,), (1,)), ((), ()))
        queries = (late_recv[:, u - len(settled)] if late else lat_recv[:, :, u]).reshape(
            unit_rows, latent
        )
        pairs = [wide(rot_recv[e, u]) for e in range(columns)]
        turns = rounded(
            jnp.concatenate(
                [
                    pairs[e][c * cut : (c + 1) * cut, s * rope : (s + 1) * rope]
                    for e in range(columns)
                    for c in range(cuts)
                    for s in range(PAIR)
                ],
                axis=0,
            )
        )
        cached = jnp.dot(
            queries, keys[k, :latent], preferred_element_type=jnp.float32
        ) + jnp.dot(turns, keys[k, latent:], preferred_element_type=jnp.float32)
        decoded = lax.dot_general(
            queries, newer[k, :, :latent], nt, preferred_element_type=jnp.float32
        ) + lax.dot_general(
            turns, newer[k, :, latent:], nt, preferred_element_type=jnp.float32
        )
        scores = jnp.concatenate([cached, decoded], axis=1)
        scores = jnp.where(token <= span * PAIR + within, scores * scale, -jnp.inf)
        spread = jnp.exp(scores - jnp.max(scores, axis=1, keepdims=True))
        weights = rounded(spread / jnp.sum(spread, axis=1, keepdims=True))
        mixed = rounded(
            lax.dot_general(
                weights[:, :capacity], keys[k, :latent], nt, preferred_element_type=jnp.float32
            )
            + jnp.dot(
                weights[:, capacity:], newer[k, :, :latent], preferred_element_type=jnp.float32
            )
        ).reshape(columns, PAIR * heads, latent)
        back_recv[u, 0] = mixed[0]
        for e in range(1, columns):
            back_send[u, e] = mixed[e]

    def project(member, c):
        span, k = member
        u = number[member]
        low, high = back_pieces[member][c] if c is not None else (0, cuts)
        for j in range(len(back_pieces[member])) if c is None else [c]:
            back_all(member, j).wait_recv()
        for e in range(columns):
            for j in range(low, high):
                value = wide(back_recv[u, e, j * per : (j + 1) * per])
                for s in range(PAIR):
                    for l in range(latent // LANES):
                        rows_mid[l, pl.ds(place(0, e, s) + j * cut, cut)] = value[
                            s * cut : (s + 1) * cut, lane(l)
                        ]

        def head(i, carry):
            at = pl.ds(i, columns * PAIR, stride=heads)
            picked = jnp.concatenate(
                [rounded(rows_mid[l, at]) for l in range(latent // LANES)], axis=1
            )
            rows_out[at] = jnp.dot(picked, wv[i], preferred_element_type=jnp.float32)
            return carry

        count = (high - low) * cut
        start = low * cut
        lax.fori_loop(start, start + count, head, 0, unroll=min(count, 8))
        for e in range(columns):
            for s in range(PAIR):
                value = rounded(rows_out[pl.ds(place(0, e, s) + start, count)])
                if member in moving:
                    home[k, s, e, start : start + count] = value
                else:
                    out_ref[span * PAIR + s, slot(e, k), start : start + count] = value

    shifts = remote(shift_of.at[others], shift_of.at[others], shift_ss, shift_rs, at_column(1))
    mines = remote(moved, moved, mine_ss, mine_rs, at_group(1))
    newers = remote(moved_key, moved_key, key_ss, key_rs, at_group(1))
    homes = remote(home_recv, home_recv, home_ss, home_rs, at_group(1))
    for copy in (shifts, mines):
        copy.wait_recv()
    turn(moving, 1)
    for e in near_up:
        rot_copy(1, e).start()
    absorb(moving, 1, lambda c: None)
    for e in near_up:
        late_copy(e).start()
    attend(first[0])

    @pl.when(jnp.logical_not(end))
    def _():
        send_back(pieces_of(first[:1], back_pieces), far_down)

    for member in settled[1:]:
        attend(member)
    newers.wait_recv()
    for k in range(movers):
        later = chosen(0, k, lambda n: moved_key[n, k])
        newer[k, 0:16] = rounded(jnp.where(row < PAIR, wide(newer[k, 0:16]), later))
    for member in moving:
        attend(member)
    send_back(pieces_of(moving, back_pieces), far_down)

    @pl.when(end)
    def _():
        send_back(pieces_of(first[:1], back_pieces), far_down)

    send_back(pieces_of(settled[1:], back_pieces), near_down[:1])
    send_back(pieces_of(first[1:], back_pieces), far_down[:-1])
    for e in far_down[:-1]:
        send_back(pieces_of(rest, back_pieces), [e])
    wv_copy.wait()
    for member in moving:
        project(member, None)
    for d in range(1, groups):
        home_copy(d).start()
    for member in first:
        project(member, None)
    for c in range(len(halves)):
        for member in rest:
            project(member, c)
    homes.wait_recv()
    for k in range(movers):
        for e in range(columns):
            for s in range(PAIR):
                out_ref[PAIR + s, slot(e, k)] = rounded(
                    chosen(e, k, lambda n: home_recv[n, k, s, e])
                )
    remote(
        rot_send.at[others], rot_recv.at[others], rot_ss, rot_rs.at[0], at_column(1)
    ).wait_send()
    remote(
        back_send.at[:, others], back_recv.at[:, others], back_ss, back_rs.at[0], at_column(1)
    ).wait_send()
    for copy in (lats, lates, shifts, mines, newers, homes):
        copy.wait_send()


def local_part(heads):
    return max(heads // 4, 1)


def cuts_of(heads):
    return 1 if heads % 32 else 4


def body(q_nope, q_rope, w_absorb_k, w_absorb_v, latent_cache, new_latent, lengths, moves):
    steps, slots, heads, width = q_nope.shape
    rope = q_rope.shape[3]
    latent = w_absorb_k.shape[2]
    holders, capacity, entries = latent_cache.shape
    movers = moves.shape[1]
    groups = lax.axis_size("grp")
    columns = lax.axis_size("head")
    scale = YARN_GAIN / math.sqrt(width + rope)
    assert steps == 2 * PAIR
    units = steps // PAIR * holders
    rows = (2 * holders - movers) * columns * PAIR * heads
    others = groups - 1
    bf16, f32 = jnp.bfloat16, jnp.float32
    dma = pltpu.SemaphoreType.DMA
    hbm = pl.BlockSpec(memory_space=pl.ANY)
    parts = heads // local_part(heads)
    cuts = cuts_of(heads)
    here = functools.partial(pltpu.with_memory_space_constraint, memory_space=pltpu.HBM)
    arrays = (
        q_nope, q_rope, new_latent, w_absorb_k, w_absorb_v, jnp.swapaxes(latent_cache, 1, 2)
    )
    return pl.pallas_call(
        functools.partial(kernel, groups, columns, scale),
        out_shape=pltpu.VMEM(q_nope.shape, bf16),
        in_specs=[hbm, pl.BlockSpec(memory_space=pltpu.SMEM)] + [hbm] * len(arrays),
        out_specs=pl.BlockSpec(memory_space=pltpu.VMEM),
        scratch_shapes=[
            pltpu.SMEM(lengths.shape, jnp.int32),
            pltpu.VMEM(q_nope.shape, bf16),
            pltpu.VMEM(q_rope.shape, bf16),
            pltpu.VMEM(new_latent.shape, bf16),
            dma((4,)),
            pltpu.VMEM(w_absorb_k.shape, bf16),
            pltpu.VMEM(w_absorb_v.shape, bf16),
            pltpu.VMEM((holders, entries, capacity), bf16),
            pltpu.VMEM((holders, EXTRA, entries), bf16),
            dma((parts + 2,)),
            pltpu.VMEM((rows, width), f32),
            pltpu.VMEM((latent // LANES, rows, LANES), f32),
            pltpu.VMEM((rows, width), f32),
            pltpu.VMEM((columns, cuts, units - movers, PAIR * heads // cuts, latent), bf16),
            pltpu.VMEM((columns, cuts, units - movers, PAIR * heads // cuts, latent), bf16),
            pltpu.VMEM((columns, movers, cuts, PAIR * heads // cuts, latent), bf16),
            pltpu.VMEM((columns, movers, cuts, PAIR * heads // cuts, latent), bf16),
            pltpu.VMEM((columns, units, heads, PAIR * rope), bf16),
            pltpu.VMEM((columns, units, heads, PAIR * rope), bf16),
            pltpu.VMEM((units, columns, PAIR * heads, latent), bf16),
            pltpu.VMEM((units, columns, PAIR * heads, latent), bf16),
            pltpu.VMEM((movers, PAIR + 1, columns, heads, width), bf16),
            pltpu.VMEM((others, movers, PAIR + 1, columns, heads, width), bf16),
            pltpu.VMEM((movers, 16, entries), bf16),
            pltpu.VMEM((others, movers, 16, entries), bf16),
            pltpu.VMEM((movers, PAIR, columns, heads, width), bf16),
            pltpu.VMEM((others, movers, PAIR, columns, heads, width), bf16),
            pltpu.VMEM((columns, movers, 8, LANES), jnp.int32),
            pltpu.VMEM((movers, 8, LANES), jnp.int32),
            dma, dma, dma, dma,
            dma, dma((2,)),
            dma, dma((2 * units,)),
            dma, dma, dma, dma, dma, dma, dma, dma,
            pltpu.SemaphoreType.REGULAR((columns - 1,)), pltpu.SemaphoreType.REGULAR,
        ],
        compiler_params=pltpu.CompilerParams(
            collective_id=0, has_side_effects=True, vmem_limit_bytes=44 << 20
        ),
    )(here(lengths), moves, *map(here, arrays))


def solution(mesh):
    placed = (
        P(None, "grp", "head", None),
        P(None, "grp", "head", None),
        P("head", None, None),
        P("head", None, None),
        P(("grp", "head"), None, None),
        P(None, ("grp", "head"), None),
        P(),
        P("head", None),
    )
    return jax.shard_map(
        body, mesh=mesh, in_specs=placed, out_specs=P(None, "grp", "head", None), check_vma=False
    )
```

```python
import functools
import math

import jax
import jax.numpy as jnp
from jax import lax
from jax.experimental import pallas as pl
from jax.experimental.pallas import tpu as pltpu
from jax.sharding import PartitionSpec as P

PAIR = 2
EXTRA = 128
LANES = 128
YARN_GAIN = (0.1 * math.log(40.0) + 1.0) ** 2
MESH = pl.DeviceIdType.MESH


def lane(c):
    return slice(c * LANES, (c + 1) * LANES)


def rounded(value):
    return value.astype(jnp.bfloat16)


def wide(value):
    return value.astype(jnp.float32)


def kernel(
    groups, columns, scale,
    length_hbm, move_ref, nope_hbm, rope_hbm, fresh_hbm, wk_hbm, wv_hbm, cache_hbm,
    out_ref,
    length_ref, nope_ref, rope_ref, fresh_ref, entry_sem,
    wk, wv, keys, newer, local_sem,
    rows_in, rows_mid, rows_out,
    lat_send, lat_recv, late_send, late_recv, rot_send, rot_recv, back_send, back_recv,
    mine, moved, mine_key, moved_key, home, home_recv, shift_of, shift_mine,
    lat_ss, lat_rs, late_ss, late_rs, rot_ss, rot_rs, back_ss, back_rs,
    mine_ss, mine_rs, key_ss, key_rs, home_ss, home_rs, shift_ss, shift_rs,
    near_sem, rank_sem,
):
    steps, _, heads, _ = nope_ref.shape
    holders, entries, capacity = cache_hbm.shape
    latent = wk.shape[2]
    rope = entries - latent
    movers = move_ref.shape[1]
    total = capacity + EXTRA
    cuts = cuts_of(heads)
    cut = heads // cuts
    rank = lax.axis_index("grp")
    column = lax.axis_index("head")
    parts = wk.shape[0] // local_part(heads)
    part = local_part(heads)

    first = [(0, k) for k in range(holders)]
    rest = [(1, k) for k in range(movers, holders)]
    moving = [(1, k) for k in range(movers)]
    settled = first + rest
    number = {member: u for u, member in enumerate(settled + moving)}

    def at_column(e):
        return (rank, lax.rem(column + e + columns, columns))

    def at_group(d):
        return (lax.rem(rank + d + groups, groups), column)

    barrier = pltpu.get_barrier_semaphore()
    for e in range(1, columns):
        @pl.when(column + e < columns)
        def _():
            pl.semaphore_signal(barrier, inc=1, device_id=at_column(e), device_id_type=MESH)

    for d in range(1, groups):
        @pl.when(rank + d < groups)
        def _():
            pl.semaphore_signal(barrier, inc=1, device_id=at_group(d), device_id_type=MESH)

    wk_copies = [
        pltpu.make_async_copy(
            wk_hbm.at[pl.ds(n * part, part)], wk.at[pl.ds(n * part, part)], local_sem.at[n]
        )
        for n in range(parts)
    ]
    key_copy = pltpu.make_async_copy(cache_hbm, keys, local_sem.at[parts])
    wv_copy = pltpu.make_async_copy(wv_hbm, wv, local_sem.at[parts + 1])
    entry_copies = [
        pltpu.make_async_copy(src, dst, entry_sem.at[n])
        for n, (src, dst) in enumerate(
            (
                (rope_hbm, rope_ref), (nope_hbm, nope_ref), (fresh_hbm, fresh_ref),
                (length_hbm, length_ref),
            )
        )
    ]
    for copy in entry_copies[:2] + wk_copies[:1]:
        copy.start()

    below = rank + column

    @pl.when(below > 0)
    def _():
        pl.semaphore_wait(barrier, below)

    for e in range(1, columns):
        @pl.when(column >= e)
        def _():
            pl.semaphore_signal(
                near_sem.at[e - 1], inc=1, device_id=at_column(-e), device_id_type=MESH
            )

    for d in range(1, groups):
        @pl.when(rank >= d)
        def _():
            pl.semaphore_signal(
                rank_sem, inc=1, device_id=at_group(-d), device_id_type=MESH
            )

    def remote(src, dst, send, recv, target):
        return pltpu.make_async_remote_copy(
            src_ref=src, dst_ref=dst, send_sem=send, recv_sem=recv,
            device_id=target, device_id_type=MESH,
        )

    def slot(e, k):
        return lax.rem(column + e, columns) * holders + k

    def turned(span, e, k):
        return jnp.concatenate(
            [rope_ref[span * PAIR + s, slot(e, k)] for s in range(PAIR)], axis=1
        )

    def shift_copy(e):
        return remote(shift_mine, shift_of.at[columns - e], shift_ss, shift_rs, at_column(e))

    def mine_copy(d):
        return remote(mine, moved.at[d - 1], mine_ss, mine_rs, at_group(-d))

    def newer_copy(d):
        return remote(mine_key, moved_key.at[d - 1], key_ss, key_rs, at_group(-d))

    def home_copy(d):
        return remote(home, home_recv.at[d - 1], home_ss, home_rs, at_group(d))

    per = PAIR * cut
    others = pl.ds(1, columns - 1)
    halves = [(0, cuts - 1), (cuts - 1, cuts)] if cuts > 1 else [(0, 1)]
    back_pieces = {member: [(0, cuts)] for member in number}
    if cuts > 1:
        for member in rest:
            back_pieces[member] = halves

    def rows_of(piece):
        return pl.ds(piece[0] * per, (piece[1] - piece[0]) * per)

    def lat_copy(e, c):
        return remote(lat_send.at[e, c], lat_recv.at[e, c], lat_ss, lat_rs, at_column(e))

    def late_copy(e):
        return remote(late_send.at[e], late_recv.at[e], late_ss, late_rs, at_column(e))

    lats = remote(lat_send.at[others], lat_recv.at[others], lat_ss, lat_rs, at_column(1))
    lates = remote(late_send.at[others], late_recv.at[others], late_ss, late_rs, at_column(1))

    def rot_copy(late, e):
        at = pl.ds(len(settled), len(moving)) if late else pl.ds(0, len(settled))
        return remote(
            rot_send.at[e, at], rot_recv.at[e, at], rot_ss, rot_rs.at[late], at_column(e)
        )

    landed = {}
    for member in settled + moving:
        for c in range(len(back_pieces[member])):
            landed[member, c] = len(landed)

    def back_copy(member, e, c):
        u = number[member]
        at = rows_of(back_pieces[member][c])
        return remote(
            back_send.at[u, e, at], back_recv.at[u, e, at], back_ss,
            back_rs.at[landed[member, c]], at_column(-e),
        )

    def back_all(member, c):
        u = number[member]
        at = rows_of(back_pieces[member][c])
        return remote(
            back_send.at[u, others, at], back_recv.at[u, others, at], back_ss,
            back_rs.at[landed[member, c]], at_column(1),
        )

    low, high = jnp.int32(0), jnp.int32(columns - 1)
    near = []
    for _ in range(columns - 1):
        above, below = high - column, column - low
        take_high = jnp.where(2 * column < columns, above >= below, above > below)
        near.insert(0, jnp.where(take_high, high, low))
        high = jnp.where(take_high, high - 1, high)
        low = jnp.where(take_high, low, low + 1)
    near_up = [lax.rem(target - column + columns, columns) for target in near]
    near_down = [lax.rem(column - target + columns, columns) for target in near]

    far_down = near_down[::-1]
    end = jnp.logical_or(column == 0, column == columns - 1)

    def send_back(pieces, order):
        for member, c in pieces:
            for e in order:
                back_copy(member, e, c).start()

    def pieces_of(members, table):
        return [(member, c) for member in members for c in range(len(table[member]))]

    def chosen(e, k, options):
        found = wide(options(0))
        for d in range(2, groups):
            is_it = shift_of[e, k, 0:1, 0:1] == d
            found = jnp.where(is_it, wide(options(d - 1)), found)
        return found

    unit_rows = columns * PAIR * heads

    def place(m, e, s):
        return ((m * columns + e) * PAIR + s) * heads

    def turn(members, late):
        for span, k in members:
            u = number[span, k]
            for e in range(columns):
                if late:
                    pair = rounded(chosen(e, k, lambda n: moved[n, k, PAIR, e]))
                else:
                    pair = turned(span, e, k)
                if e:
                    rot_send[e, u] = pair
                else:
                    rot_recv[0, u] = pair

    def absorb(members, late, after):
        count = len(members) * columns * PAIR
        for m, (span, k) in enumerate(members):
            for e in range(columns):
                for s in range(PAIR):
                    if late:
                        value = chosen(e, k, lambda n: moved[n, k, s, e])
                    else:
                        value = wide(nope_ref[span * PAIR + s, slot(e, k)])
                    rows_in[pl.ds(place(m, e, s), heads)] = value
        for n in range(parts):
            if not late:
                wk_copies[n].wait()

            def head(i, carry):
                picked = rounded(rows_in[pl.ds(i, count, stride=heads)])
                result = jnp.dot(picked, wk[i], preferred_element_type=jnp.float32)
                for c in range(latent // LANES):
                    rows_mid[c, pl.ds(i, count, stride=heads)] = result[:, lane(c)]
                return carry

            lax.fori_loop(n * part, (n + 1) * part, head, 0, unroll=True)
            if (n + 1) % (parts // cuts):
                continue
            c = n // (parts // cuts)
            for m, member in enumerate(members):
                u = number[member]
                for e in range(columns):
                    value = rounded(
                        jnp.concatenate(
                            [
                                jnp.concatenate(
                                    [
                                        rows_mid[l, pl.ds(place(m, e, s) + c * cut, cut)]
                                        for l in range(latent // LANES)
                                    ],
                                    axis=1,
                                )
                                for s in range(PAIR)
                            ],
                            axis=0,
                        )
                    )
                    if late:
                        to, at = (late_send if e else late_recv), (e, m, c)
                    else:
                        to, at = (lat_send if e else lat_recv), (e, c, m)
                    to[at] = value
            after(c)

    entry_copies[0].wait()
    for copy in wk_copies[1:] + entry_copies[2:]:
        copy.start()
    turn(settled, 0)
    for k in range(movers):
        shift_mine[k] = jnp.full(shift_mine.shape[1:], move_ref[0, k], jnp.int32)
        shift_of[0, k] = jnp.full(shift_mine.shape[1:], move_ref[0, k], jnp.int32)
    for e in range(1, columns):
        @pl.when(column + e >= columns)
        def _():
            rot_copy(0, e).start()
            shift_copy(e).start()

    entry_copies[1].wait()
    row = lax.broadcasted_iota(jnp.int32, (16, entries), 0)

    def fresh_rows(k):
        found = jnp.zeros((16, entries), jnp.float32)
        for j in range(steps):
            found = jnp.where(row == j, wide(fresh_ref[j])[k : k + 1], found)
        return found

    def after_settled(c):
        asked = 0
        for e in range(1, columns):
            @pl.when(column + e >= columns)
            def _():
                lat_copy(e, c).start()

            if c == asked:
                @pl.when(column + e < columns)
                def _():
                    pl.semaphore_wait(near_sem.at[e - 1], 1)
                    rot_copy(0, e).start()
                    shift_copy(e).start()

        if c >= asked:
            for e in range(1, columns):
                @pl.when(column + e < columns)
                def _():
                    for j in range(c + 1) if c == asked else [c]:
                        lat_copy(e, j).start()

        if c == 0:
            for copy in entry_copies[2:]:
                copy.wait()
            for k in range(movers):
                for e in range(columns):
                    for s in range(PAIR):
                        mine[k, s, e] = nope_ref[PAIR + s, slot(e, k)]
                    mine[k, PAIR, e] = turned(1, e, k)
                mine_key[k] = rounded(fresh_rows(k))

        if c == cuts - 1:
            @pl.when(rank < groups - 1)
            def _():
                pl.semaphore_wait(rank_sem, groups - 1 - rank)

            for d in range(1, groups):
                mine_copy(d).start()
            for d in range(1, groups):
                newer_copy(d).start()

    absorb(settled, 0, after_settled)
    key_copy.start()
    wv_copy.start()
    for k in range(holders):
        newer[k] = jnp.zeros((EXTRA, entries), jnp.bfloat16)
        newer[k, 0:16] = rounded(fresh_rows(k))
    key_copy.wait()

    at_key = lax.broadcasted_iota(jnp.int32, (1, total), 1)
    at_row = lax.broadcasted_iota(jnp.int32, (unit_rows, 1), 0)
    within = lax.rem(lax.div(at_row, cut), PAIR)
    turns_in = set()

    def attend(member):
        span, k = member
        u = number[member]
        late = int(member in moving)
        if late not in turns_in:
            (lates if late else lats).wait_recv()
        if late not in turns_in:
            at = pl.ds(len(settled), len(moving)) if late else pl.ds(0, len(settled))
            remote(
                rot_send.at[others, at], rot_recv.at[others, at], rot_ss, rot_rs.at[late],
                at_column(1),
            ).wait_recv()
        turns_in.add(late)
        live = length_ref[(rank * columns + column) * holders + k]
        token = jnp.where(at_key < capacity, steps, at_key - capacity)
        token = jnp.where(at_key < live, -1, token)
        nt = (((1,), (1,)), ((), ()))
        queries = (late_recv[:, u - len(settled)] if late else lat_recv[:, :, u]).reshape(
            unit_rows, latent
        )
        pairs = [wide(rot_recv[e, u]) for e in range(columns)]
        turns = rounded(
            jnp.concatenate(
                [
                    pairs[e][c * cut : (c + 1) * cut, s * rope : (s + 1) * rope]
                    for e in range(columns)
                    for c in range(cuts)
                    for s in range(PAIR)
                ],
                axis=0,
            )
        )
        cached = jnp.dot(
            queries, keys[k, :latent], preferred_element_type=jnp.float32
        ) + jnp.dot(turns, keys[k, latent:], preferred_element_type=jnp.float32)
        decoded = lax.dot_general(
            queries, newer[k, :, :latent], nt, preferred_element_type=jnp.float32
        ) + lax.dot_general(
            turns, newer[k, :, latent:], nt, preferred_element_type=jnp.float32
        )
        scores = jnp.concatenate([cached, decoded], axis=1)
        scores = jnp.where(token <= span * PAIR + within, scores * scale, -jnp.inf)
        spread = jnp.exp(scores - jnp.max(scores, axis=1, keepdims=True))
        weights = rounded(spread / jnp.sum(spread, axis=1, keepdims=True))
        mixed = rounded(
            lax.dot_general(
                weights[:, :capacity], keys[k, :latent], nt, preferred_element_type=jnp.float32
            )
            + jnp.dot(
                weights[:, capacity:], newer[k, :, :latent], preferred_element_type=jnp.float32
            )
        ).reshape(columns, PAIR * heads, latent)
        back_recv[u, 0] = mixed[0]
        for e in range(1, columns):
            back_send[u, e] = mixed[e]

    def project(member, c):
        span, k = member
        u = number[member]
        low, high = back_pieces[member][c] if c is not None else (0, cuts)
        for j in range(len(back_pieces[member])) if c is None else [c]:
            back_all(member, j).wait_recv()
        for e in range(columns):
            for j in range(low, high):
                value = wide(back_recv[u, e, j * per : (j + 1) * per])
                for s in range(PAIR):
                    for l in range(latent // LANES):
                        rows_mid[l, pl.ds(place(0, e, s) + j * cut, cut)] = value[
                            s * cut : (s + 1) * cut, lane(l)
                        ]

        def head(i, carry):
            at = pl.ds(i, columns * PAIR, stride=heads)
            picked = jnp.concatenate(
                [rounded(rows_mid[l, at]) for l in range(latent // LANES)], axis=1
            )
            rows_out[at] = jnp.dot(picked, wv[i], preferred_element_type=jnp.float32)
            return carry

        count = (high - low) * cut
        start = low * cut
        lax.fori_loop(start, start + count, head, 0, unroll=min(count, 8))
        for e in range(columns):
            for s in range(PAIR):
                value = rounded(rows_out[pl.ds(place(0, e, s) + start, count)])
                if member in moving:
                    home[k, s, e, start : start + count] = value
                else:
                    out_ref[span * PAIR + s, slot(e, k), start : start + count] = value

    shifts = remote(shift_of.at[others], shift_of.at[others], shift_ss, shift_rs, at_column(1))
    mines = remote(moved, moved, mine_ss, mine_rs, at_group(1))
    newers = remote(moved_key, moved_key, key_ss, key_rs, at_group(1))
    homes = remote(home_recv, home_recv, home_ss, home_rs, at_group(1))
    for copy in (shifts, mines):
        copy.wait_recv()
    turn(moving, 1)
    for e in near_up:
        rot_copy(1, e).start()
    absorb(moving, 1, lambda c: None)
    for e in near_up:
        late_copy(e).start()
    attend(first[0])

    @pl.when(jnp.logical_not(end))
    def _():
        send_back(pieces_of(first[:1], back_pieces), far_down)

    newers.wait_recv()
    for k in range(movers):
        later = chosen(0, k, lambda n: moved_key[n, k])
        newer[k, 0:16] = rounded(jnp.where(row < PAIR, wide(newer[k, 0:16]), later))
    for member in moving:
        attend(member)
    send_back(pieces_of(moving, back_pieces), far_down)

    @pl.when(end)
    def _():
        send_back(pieces_of(first[:1], back_pieces), far_down)

    for member in settled[1:]:
        attend(member)
    send_back(pieces_of(settled[1:], back_pieces), near_down[:1])
    send_back(pieces_of(first[1:], back_pieces), far_down[:-1])
    for e in far_down[:-1]:
        send_back(pieces_of(rest, back_pieces), [e])
    wv_copy.wait()
    for member in moving:
        project(member, None)
    for d in range(1, groups):
        home_copy(d).start()
    for member in first:
        project(member, None)
    for c in range(len(halves)):
        for member in rest:
            project(member, c)
    homes.wait_recv()
    for k in range(movers):
        for e in range(columns):
            for s in range(PAIR):
                out_ref[PAIR + s, slot(e, k)] = rounded(
                    chosen(e, k, lambda n: home_recv[n, k, s, e])
                )
    remote(
        rot_send.at[others], rot_recv.at[others], rot_ss, rot_rs.at[0], at_column(1)
    ).wait_send()
    remote(
        back_send.at[:, others], back_recv.at[:, others], back_ss, back_rs.at[0], at_column(1)
    ).wait_send()
    for copy in (lats, lates, shifts, mines, newers, homes):
        copy.wait_send()


def local_part(heads):
    return max(heads // 4, 1)


def cuts_of(heads):
    return 1 if heads % 32 else 4


def body(q_nope, q_rope, w_absorb_k, w_absorb_v, latent_cache, new_latent, lengths, moves):
    steps, slots, heads, width = q_nope.shape
    rope = q_rope.shape[3]
    latent = w_absorb_k.shape[2]
    holders, capacity, entries = latent_cache.shape
    movers = moves.shape[1]
    groups = lax.axis_size("grp")
    columns = lax.axis_size("head")
    scale = YARN_GAIN / math.sqrt(width + rope)
    assert steps == 2 * PAIR
    units = steps // PAIR * holders
    rows = (2 * holders - movers) * columns * PAIR * heads
    others = groups - 1
    bf16, f32 = jnp.bfloat16, jnp.float32
    dma = pltpu.SemaphoreType.DMA
    hbm = pl.BlockSpec(memory_space=pl.ANY)
    parts = heads // local_part(heads)
    cuts = cuts_of(heads)
    here = functools.partial(pltpu.with_memory_space_constraint, memory_space=pltpu.HBM)
    arrays = (
        q_nope, q_rope, new_latent, w_absorb_k, w_absorb_v, jnp.swapaxes(latent_cache, 1, 2)
    )
    return pl.pallas_call(
        functools.partial(kernel, groups, columns, scale),
        out_shape=pltpu.VMEM(q_nope.shape, bf16),
        in_specs=[hbm, pl.BlockSpec(memory_space=pltpu.SMEM)] + [hbm] * len(arrays),
        out_specs=pl.BlockSpec(memory_space=pltpu.VMEM),
        scratch_shapes=[
            pltpu.SMEM(lengths.shape, jnp.int32),
            pltpu.VMEM(q_nope.shape, bf16),
            pltpu.VMEM(q_rope.shape, bf16),
            pltpu.VMEM(new_latent.shape, bf16),
            dma((4,)),
            pltpu.VMEM(w_absorb_k.shape, bf16),
            pltpu.VMEM(w_absorb_v.shape, bf16),
            pltpu.VMEM((holders, entries, capacity), bf16),
            pltpu.VMEM((holders, EXTRA, entries), bf16),
            dma((parts + 2,)),
            pltpu.VMEM((rows, width), f32),
            pltpu.VMEM((latent // LANES, rows, LANES), f32),
            pltpu.VMEM((rows, width), f32),
            pltpu.VMEM((columns, cuts, units - movers, PAIR * heads // cuts, latent), bf16),
            pltpu.VMEM((columns, cuts, units - movers, PAIR * heads // cuts, latent), bf16),
            pltpu.VMEM((columns, movers, cuts, PAIR * heads // cuts, latent), bf16),
            pltpu.VMEM((columns, movers, cuts, PAIR * heads // cuts, latent), bf16),
            pltpu.VMEM((columns, units, heads, PAIR * rope), bf16),
            pltpu.VMEM((columns, units, heads, PAIR * rope), bf16),
            pltpu.VMEM((units, columns, PAIR * heads, latent), bf16),
            pltpu.VMEM((units, columns, PAIR * heads, latent), bf16),
            pltpu.VMEM((movers, PAIR + 1, columns, heads, width), bf16),
            pltpu.VMEM((others, movers, PAIR + 1, columns, heads, width), bf16),
            pltpu.VMEM((movers, 16, entries), bf16),
            pltpu.VMEM((others, movers, 16, entries), bf16),
            pltpu.VMEM((movers, PAIR, columns, heads, width), bf16),
            pltpu.VMEM((others, movers, PAIR, columns, heads, width), bf16),
            pltpu.VMEM((columns, movers, 8, LANES), jnp.int32),
            pltpu.VMEM((movers, 8, LANES), jnp.int32),
            dma, dma, dma, dma,
            dma, dma((2,)),
            dma, dma((2 * units,)),
            dma, dma, dma, dma, dma, dma, dma, dma,
            pltpu.SemaphoreType.REGULAR((columns - 1,)), pltpu.SemaphoreType.REGULAR,
        ],
        compiler_params=pltpu.CompilerParams(
            collective_id=0, has_side_effects=True, vmem_limit_bytes=44 << 20
        ),
    )(here(lengths), moves, *map(here, arrays))


def solution(mesh):
    placed = (
        P(None, "grp", "head", None),
        P(None, "grp", "head", None),
        P("head", None, None),
        P("head", None, None),
        P(("grp", "head"), None, None),
        P(None, ("grp", "head"), None),
        P(),
        P("head", None),
    )
    return jax.shard_map(
        body, mesh=mesh, in_specs=placed, out_specs=P(None, "grp", "head", None), check_vma=False
    )
```

```python
import functools
import math

import jax
import jax.numpy as jnp
from jax import lax
from jax.experimental import pallas as pl
from jax.experimental.pallas import tpu as pltpu
from jax.sharding import PartitionSpec as P

PAIR = 2
EXTRA = 128
LANES = 128
YARN_GAIN = (0.1 * math.log(40.0) + 1.0) ** 2
MESH = pl.DeviceIdType.MESH


def lane(c):
    return slice(c * LANES, (c + 1) * LANES)


def rounded(value):
    return value.astype(jnp.bfloat16)


def wide(value):
    return value.astype(jnp.float32)


def kernel(
    groups, columns, scale,
    length_hbm, move_ref, nope_hbm, rope_hbm, fresh_hbm, wk_hbm, wv_hbm, cache_hbm,
    out_ref,
    length_ref, nope_ref, rope_ref, fresh_ref, entry_sem,
    wk, wv, keys, newer, local_sem,
    rows_in, rows_mid, rows_out,
    lat_send, lat_recv, late_send, late_recv, rot_send, rot_recv, back_send, back_recv,
    mine, moved, mine_key, moved_key, home, home_recv, shift_of, shift_mine,
    lat_ss, lat_rs, late_ss, late_rs, rot_ss, rot_rs, back_ss, back_rs,
    mine_ss, mine_rs, key_ss, key_rs, home_ss, home_rs, shift_ss, shift_rs,
    near_sem, rank_sem, open_sem,
):
    steps, _, heads, _ = nope_ref.shape
    holders, entries, capacity = cache_hbm.shape
    latent = wk.shape[2]
    rope = entries - latent
    movers = move_ref.shape[1]
    total = capacity + EXTRA
    cuts = cuts_of(heads)
    cut = heads // cuts
    rank = lax.axis_index("grp")
    column = lax.axis_index("head")
    parts = wk.shape[0] // local_part(heads)
    part = local_part(heads)

    first = [(0, k) for k in range(holders)]
    rest = [(1, k) for k in range(movers, holders)]
    moving = [(1, k) for k in range(movers)]
    settled = first + rest
    number = {member: u for u, member in enumerate(settled + moving)}

    def at_column(e):
        return (rank, lax.rem(column + e + columns, columns))

    def at_group(d):
        return (lax.rem(rank + d + groups, groups), column)

    barrier = pltpu.get_barrier_semaphore()
    for e in range(1, columns):
        @pl.when(column + e < columns)
        def _():
            pl.semaphore_signal(barrier, inc=1, device_id=at_column(e), device_id_type=MESH)

    @pl.when(rank == 0)
    def _():
        for d in range(1, groups):
            pl.semaphore_signal(barrier, inc=1, device_id=at_group(d), device_id_type=MESH)

    wk_copies = [
        pltpu.make_async_copy(
            wk_hbm.at[pl.ds(n * part, part)], wk.at[pl.ds(n * part, part)], local_sem.at[n]
        )
        for n in range(parts)
    ]
    key_copy = pltpu.make_async_copy(cache_hbm, keys, local_sem.at[parts])
    wv_copy = pltpu.make_async_copy(wv_hbm, wv, local_sem.at[parts + 1])
    entry_copies = [
        pltpu.make_async_copy(src, dst, entry_sem.at[n])
        for n, (src, dst) in enumerate(
            (
                (rope_hbm, rope_ref), (nope_hbm, nope_ref), (fresh_hbm, fresh_ref),
                (length_hbm, length_ref),
            )
        )
    ]
    for copy in entry_copies[:2] + wk_copies[:1]:
        copy.start()

    below = column + jnp.minimum(rank, 1)

    @pl.when(below > 0)
    def _():
        pl.semaphore_wait(barrier, below)

    for e in range(1, columns):
        @pl.when(column >= e)
        def _():
            pl.semaphore_signal(
                near_sem.at[e - 1], inc=1, device_id=at_column(-e), device_id_type=MESH
            )

    @pl.when(rank > 0)
    def _():
        pl.semaphore_signal(rank_sem, inc=1, device_id=(0, column), device_id_type=MESH)

    def remote(src, dst, send, recv, target):
        return pltpu.make_async_remote_copy(
            src_ref=src, dst_ref=dst, send_sem=send, recv_sem=recv,
            device_id=target, device_id_type=MESH,
        )

    def slot(e, k):
        return lax.rem(column + e, columns) * holders + k

    def turned(span, e, k):
        return jnp.concatenate(
            [rope_ref[span * PAIR + s, slot(e, k)] for s in range(PAIR)], axis=1
        )

    def shift_copy(e):
        return remote(shift_mine, shift_of.at[columns - e], shift_ss, shift_rs, at_column(e))

    def mine_copy(d):
        return remote(mine, moved.at[d - 1], mine_ss, mine_rs, at_group(-d))

    def newer_copy(d):
        return remote(mine_key, moved_key.at[d - 1], key_ss, key_rs, at_group(-d))

    def home_copy(d):
        return remote(home, home_recv.at[d - 1], home_ss, home_rs, at_group(d))

    per = PAIR * cut
    others = pl.ds(1, columns - 1)
    halves = [(0, cuts - 1), (cuts - 1, cuts)] if cuts > 1 else [(0, 1)]
    back_pieces = {member: [(0, cuts)] for member in number}
    if cuts > 1:
        for member in rest:
            back_pieces[member] = halves

    def rows_of(piece):
        return pl.ds(piece[0] * per, (piece[1] - piece[0]) * per)

    def lat_copy(e, c):
        return remote(lat_send.at[e, c], lat_recv.at[e, c], lat_ss, lat_rs, at_column(e))

    def late_copy(e):
        return remote(late_send.at[e], late_recv.at[e], late_ss, late_rs, at_column(e))

    lats = remote(lat_send.at[others], lat_recv.at[others], lat_ss, lat_rs, at_column(1))
    lates = remote(late_send.at[others], late_recv.at[others], late_ss, late_rs, at_column(1))

    def rot_copy(late, e):
        at = pl.ds(len(settled), len(moving)) if late else pl.ds(0, len(settled))
        return remote(
            rot_send.at[e, at], rot_recv.at[e, at], rot_ss, rot_rs.at[late], at_column(e)
        )

    landed = {}
    for member in settled + moving:
        for c in range(len(back_pieces[member])):
            landed[member, c] = len(landed)

    def back_copy(member, e, c):
        u = number[member]
        at = rows_of(back_pieces[member][c])
        return remote(
            back_send.at[u, e, at], back_recv.at[u, e, at], back_ss,
            back_rs.at[landed[member, c]], at_column(-e),
        )

    def back_all(member, c):
        u = number[member]
        at = rows_of(back_pieces[member][c])
        return remote(
            back_send.at[u, others, at], back_recv.at[u, others, at], back_ss,
            back_rs.at[landed[member, c]], at_column(1),
        )

    low, high = jnp.int32(0), jnp.int32(columns - 1)
    near = []
    for _ in range(columns - 1):
        above, below = high - column, column - low
        take_high = jnp.where(2 * column < columns, above >= below, above > below)
        near.insert(0, jnp.where(take_high, high, low))
        high = jnp.where(take_high, high - 1, high)
        low = jnp.where(take_high, low, low + 1)
    near_up = [lax.rem(target - column + columns, columns) for target in near]
    near_down = [lax.rem(column - target + columns, columns) for target in near]

    far_down = near_down[::-1]
    end = jnp.logical_or(column == 0, column == columns - 1)

    def send_back(pieces, order):
        for member, c in pieces:
            for e in order:
                back_copy(member, e, c).start()

    def pieces_of(members, table):
        return [(member, c) for member in members for c in range(len(table[member]))]

    def chosen(e, k, options):
        found = wide(options(0))
        for d in range(2, groups):
            is_it = shift_of[e, k, 0:1, 0:1] == d
            found = jnp.where(is_it, wide(options(d - 1)), found)
        return found

    unit_rows = columns * PAIR * heads

    def place(m, e, s):
        return ((m * columns + e) * PAIR + s) * heads

    def turn(members, late):
        for span, k in members:
            u = number[span, k]
            for e in range(columns):
                if late:
                    pair = rounded(chosen(e, k, lambda n: moved[n, k, PAIR, e]))
                else:
                    pair = turned(span, e, k)
                if e:
                    rot_send[e, u] = pair
                else:
                    rot_recv[0, u] = pair

    def absorb(members, late, after):
        count = len(members) * columns * PAIR
        for m, (span, k) in enumerate(members):
            for e in range(columns):
                for s in range(PAIR):
                    if late:
                        value = chosen(e, k, lambda n: moved[n, k, s, e])
                    else:
                        value = wide(nope_ref[span * PAIR + s, slot(e, k)])
                    rows_in[pl.ds(place(m, e, s), heads)] = value
        for n in range(parts):
            if not late:
                wk_copies[n].wait()

            def head(i, carry):
                picked = rounded(rows_in[pl.ds(i, count, stride=heads)])
                result = jnp.dot(picked, wk[i], preferred_element_type=jnp.float32)
                for c in range(latent // LANES):
                    rows_mid[c, pl.ds(i, count, stride=heads)] = result[:, lane(c)]
                return carry

            lax.fori_loop(n * part, (n + 1) * part, head, 0, unroll=True)
            if (n + 1) % (parts // cuts):
                continue
            c = n // (parts // cuts)
            for m, member in enumerate(members):
                u = number[member]
                for e in range(columns):
                    value = rounded(
                        jnp.concatenate(
                            [
                                jnp.concatenate(
                                    [
                                        rows_mid[l, pl.ds(place(m, e, s) + c * cut, cut)]
                                        for l in range(latent // LANES)
                                    ],
                                    axis=1,
                                )
                                for s in range(PAIR)
                            ],
                            axis=0,
                        )
                    )
                    if late:
                        to, at = (late_send if e else late_recv), (e, m, c)
                    else:
                        to, at = (lat_send if e else lat_recv), (e, c, m)
                    to[at] = value
            after(c)

    entry_copies[0].wait()
    for copy in wk_copies[1:] + entry_copies[2:]:
        copy.start()
    turn(settled, 0)
    for k in range(movers):
        shift_mine[k] = jnp.full(shift_mine.shape[1:], move_ref[0, k], jnp.int32)
        shift_of[0, k] = jnp.full(shift_mine.shape[1:], move_ref[0, k], jnp.int32)
    for e in range(1, columns):
        @pl.when(column + e >= columns)
        def _():
            rot_copy(0, e).start()
            shift_copy(e).start()

    entry_copies[1].wait()
    row = lax.broadcasted_iota(jnp.int32, (16, entries), 0)

    def fresh_rows(k):
        found = jnp.zeros((16, entries), jnp.float32)
        for j in range(steps):
            found = jnp.where(row == j, wide(fresh_ref[j])[k : k + 1], found)
        return found

    def after_settled(c):
        asked = 0
        for e in range(1, columns):
            @pl.when(column + e >= columns)
            def _():
                lat_copy(e, c).start()

            if c == asked:
                @pl.when(column + e < columns)
                def _():
                    pl.semaphore_wait(near_sem.at[e - 1], 1)
                    rot_copy(0, e).start()
                    shift_copy(e).start()

        if c >= asked:
            for e in range(1, columns):
                @pl.when(column + e < columns)
                def _():
                    for j in range(c + 1) if c == asked else [c]:
                        lat_copy(e, j).start()

        if c == 0:
            for copy in entry_copies[2:]:
                copy.wait()
            for k in range(movers):
                for e in range(columns):
                    for s in range(PAIR):
                        mine[k, s, e] = nope_ref[PAIR + s, slot(e, k)]
                    mine[k, PAIR, e] = turned(1, e, k)
                mine_key[k] = rounded(fresh_rows(k))

        if c == cuts - 1:
            @pl.when(rank == 0)
            def _():
                pl.semaphore_wait(rank_sem, groups - 1)
                for d in range(1, groups):
                    pl.semaphore_signal(
                        open_sem, inc=1, device_id=at_group(d), device_id_type=MESH
                    )

            @pl.when(rank > 0)
            def _():
                pl.semaphore_wait(open_sem, 1)

            for d in range(1, groups):
                mine_copy(d).start()
            for d in range(1, groups):
                newer_copy(d).start()

    absorb(settled, 0, after_settled)
    key_copy.start()
    wv_copy.start()
    for k in range(holders):
        newer[k] = jnp.zeros((EXTRA, entries), jnp.bfloat16)
        newer[k, 0:16] = rounded(fresh_rows(k))
    key_copy.wait()

    at_key = lax.broadcasted_iota(jnp.int32, (1, total), 1)
    at_row = lax.broadcasted_iota(jnp.int32, (unit_rows, 1), 0)
    within = lax.rem(lax.div(at_row, cut), PAIR)
    turns_in = set()

    def attend(member):
        span, k = member
        u = number[member]
        late = int(member in moving)
        if late not in turns_in:
            (lates if late else lats).wait_recv()
        if late not in turns_in:
            at = pl.ds(len(settled), len(moving)) if late else pl.ds(0, len(settled))
            remote(
                rot_send.at[others, at], rot_recv.at[others, at], rot_ss, rot_rs.at[late],
                at_column(1),
            ).wait_recv()
        turns_in.add(late)
        live = length_ref[(rank * columns + column) * holders + k]
        token = jnp.where(at_key < capacity, steps, at_key - capacity)
        token = jnp.where(at_key < live, -1, token)
        nt = (((1,), (1,)), ((), ()))
        queries = (late_recv[:, u - len(settled)] if late else lat_recv[:, :, u]).reshape(
            unit_rows, latent
        )
        pairs = [wide(rot_recv[e, u]) for e in range(columns)]
        turns = rounded(
            jnp.concatenate(
                [
                    pairs[e][c * cut : (c + 1) * cut, s * rope : (s + 1) * rope]
                    for e in range(columns)
                    for c in range(cuts)
                    for s in range(PAIR)
                ],
                axis=0,
            )
        )
        cached = jnp.dot(
            queries, keys[k, :latent], preferred_element_type=jnp.float32
        ) + jnp.dot(turns, keys[k, latent:], preferred_element_type=jnp.float32)
        decoded = lax.dot_general(
            queries, newer[k, :, :latent], nt, preferred_element_type=jnp.float32
        ) + lax.dot_general(
            turns, newer[k, :, latent:], nt, preferred_element_type=jnp.float32
        )
        scores = jnp.concatenate([cached, decoded], axis=1)
        scores = jnp.where(token <= span * PAIR + within, scores * scale, -jnp.inf)
        spread = jnp.exp(scores - jnp.max(scores, axis=1, keepdims=True))
        weights = rounded(spread / jnp.sum(spread, axis=1, keepdims=True))
        mixed = rounded(
            lax.dot_general(
                weights[:, :capacity], keys[k, :latent], nt, preferred_element_type=jnp.float32
            )
            + jnp.dot(
                weights[:, capacity:], newer[k, :, :latent], preferred_element_type=jnp.float32
            )
        ).reshape(columns, PAIR * heads, latent)
        back_recv[u, 0] = mixed[0]
        for e in range(1, columns):
            back_send[u, e] = mixed[e]

    def project(member, c):
        span, k = member
        u = number[member]
        low, high = back_pieces[member][c] if c is not None else (0, cuts)
        for j in range(len(back_pieces[member])) if c is None else [c]:
            back_all(member, j).wait_recv()
        for e in range(columns):
            for j in range(low, high):
                value = wide(back_recv[u, e, j * per : (j + 1) * per])
                for s in range(PAIR):
                    for l in range(latent // LANES):
                        rows_mid[l, pl.ds(place(0, e, s) + j * cut, cut)] = value[
                            s * cut : (s + 1) * cut, lane(l)
                        ]

        def head(i, carry):
            at = pl.ds(i, columns * PAIR, stride=heads)
            picked = jnp.concatenate(
                [rounded(rows_mid[l, at]) for l in range(latent // LANES)], axis=1
            )
            rows_out[at] = jnp.dot(picked, wv[i], preferred_element_type=jnp.float32)
            return carry

        count = (high - low) * cut
        start = low * cut
        lax.fori_loop(start, start + count, head, 0, unroll=True)
        for e in range(columns):
            for s in range(PAIR):
                value = rounded(rows_out[pl.ds(place(0, e, s) + start, count)])
                if member in moving:
                    home[k, s, e, start : start + count] = value
                else:
                    out_ref[span * PAIR + s, slot(e, k), start : start + count] = value

    shifts = remote(shift_of.at[others], shift_of.at[others], shift_ss, shift_rs, at_column(1))
    mines = remote(moved, moved, mine_ss, mine_rs, at_group(1))
    newers = remote(moved_key, moved_key, key_ss, key_rs, at_group(1))
    homes = remote(home_recv, home_recv, home_ss, home_rs, at_group(1))
    for copy in (shifts, mines):
        copy.wait_recv()
    turn(moving, 1)
    for e in near_up:
        rot_copy(1, e).start()
    absorb(moving, 1, lambda c: None)
    for e in near_up:
        late_copy(e).start()
    attend(first[0])

    @pl.when(jnp.logical_not(end))
    def _():
        send_back(pieces_of(first[:1], back_pieces), far_down)

    newers.wait_recv()
    for k in range(movers):
        later = chosen(0, k, lambda n: moved_key[n, k])
        newer[k, 0:16] = rounded(jnp.where(row < PAIR, wide(newer[k, 0:16]), later))
    for member in moving:
        attend(member)
    send_back(pieces_of(moving, back_pieces), far_down)

    @pl.when(end)
    def _():
        send_back(pieces_of(first[:1], back_pieces), far_down)

    for member in settled[1:]:
        attend(member)
    odd = lax.rem(rank, 2) == 1
    past = [jnp.where(odd, a, b) for a, b in zip(near_down[1:], far_down[:-1])]
    send_back(pieces_of(settled[1:], back_pieces), near_down[:1])
    upper = jnp.logical_and(2 * column >= columns, jnp.logical_not(odd))

    @pl.when(upper)
    def _():
        for e in past:
            send_back(pieces_of(settled[1:], back_pieces), [e])

    @pl.when(jnp.logical_not(upper))
    def _():
        send_back(pieces_of(first[1:], back_pieces), past)
        for e in past:
            send_back(pieces_of(rest, back_pieces), [e])
    wv_copy.wait()
    for member in moving:
        project(member, None)
    for d in range(1, groups):
        home_copy(d).start()
    for member in first:
        project(member, None)
    for c in range(len(halves)):
        for member in rest:
            project(member, c)
    homes.wait_recv()
    for k in range(movers):
        for e in range(columns):
            for s in range(PAIR):
                out_ref[PAIR + s, slot(e, k)] = rounded(
                    chosen(e, k, lambda n: home_recv[n, k, s, e])
                )
    remote(
        rot_send.at[others], rot_recv.at[others], rot_ss, rot_rs.at[0], at_column(1)
    ).wait_send()
    remote(
        back_send.at[:, others], back_recv.at[:, others], back_ss, back_rs.at[0], at_column(1)
    ).wait_send()
    for copy in (lats, lates, shifts, mines, newers, homes):
        copy.wait_send()


def local_part(heads):
    return max(heads // 4, 1)


def cuts_of(heads):
    return 1 if heads % 32 else 4


def body(q_nope, q_rope, w_absorb_k, w_absorb_v, latent_cache, new_latent, lengths, moves):
    steps, slots, heads, width = q_nope.shape
    rope = q_rope.shape[3]
    latent = w_absorb_k.shape[2]
    holders, capacity, entries = latent_cache.shape
    movers = moves.shape[1]
    groups = lax.axis_size("grp")
    columns = lax.axis_size("head")
    scale = YARN_GAIN / math.sqrt(width + rope)
    assert steps == 2 * PAIR
    units = steps // PAIR * holders
    rows = (2 * holders - movers) * columns * PAIR * heads
    others = groups - 1
    bf16, f32 = jnp.bfloat16, jnp.float32
    dma = pltpu.SemaphoreType.DMA
    hbm = pl.BlockSpec(memory_space=pl.ANY)
    parts = heads // local_part(heads)
    cuts = cuts_of(heads)
    here = functools.partial(pltpu.with_memory_space_constraint, memory_space=pltpu.HBM)
    arrays = (
        q_nope, q_rope, new_latent, w_absorb_k, w_absorb_v, jnp.swapaxes(latent_cache, 1, 2)
    )
    return pl.pallas_call(
        functools.partial(kernel, groups, columns, scale),
        out_shape=pltpu.VMEM(q_nope.shape, bf16),
        in_specs=[hbm, pl.BlockSpec(memory_space=pltpu.SMEM)] + [hbm] * len(arrays),
        out_specs=pl.BlockSpec(memory_space=pltpu.VMEM),
        scratch_shapes=[
            pltpu.SMEM(lengths.shape, jnp.int32),
            pltpu.VMEM(q_nope.shape, bf16),
            pltpu.VMEM(q_rope.shape, bf16),
            pltpu.VMEM(new_latent.shape, bf16),
            dma((4,)),
            pltpu.VMEM(w_absorb_k.shape, bf16),
            pltpu.VMEM(w_absorb_v.shape, bf16),
            pltpu.VMEM((holders, entries, capacity), bf16),
            pltpu.VMEM((holders, EXTRA, entries), bf16),
            dma((parts + 2,)),
            pltpu.VMEM((rows, width), f32),
            pltpu.VMEM((latent // LANES, rows, LANES), f32),
            pltpu.VMEM((rows, width), f32),
            pltpu.VMEM((columns, cuts, units - movers, PAIR * heads // cuts, latent), bf16),
            pltpu.VMEM((columns, cuts, units - movers, PAIR * heads // cuts, latent), bf16),
            pltpu.VMEM((columns, movers, cuts, PAIR * heads // cuts, latent), bf16),
            pltpu.VMEM((columns, movers, cuts, PAIR * heads // cuts, latent), bf16),
            pltpu.VMEM((columns, units, heads, PAIR * rope), bf16),
            pltpu.VMEM((columns, units, heads, PAIR * rope), bf16),
            pltpu.VMEM((units, columns, PAIR * heads, latent), bf16),
            pltpu.VMEM((units, columns, PAIR * heads, latent), bf16),
            pltpu.VMEM((movers, PAIR + 1, columns, heads, width), bf16),
            pltpu.VMEM((others, movers, PAIR + 1, columns, heads, width), bf16),
            pltpu.VMEM((movers, 16, entries), bf16),
            pltpu.VMEM((others, movers, 16, entries), bf16),
            pltpu.VMEM((movers, PAIR, columns, heads, width), bf16),
            pltpu.VMEM((others, movers, PAIR, columns, heads, width), bf16),
            pltpu.VMEM((columns, movers, 8, LANES), jnp.int32),
            pltpu.VMEM((movers, 8, LANES), jnp.int32),
            dma, dma, dma, dma,
            dma, dma((2,)),
            dma, dma((2 * units,)),
            dma, dma, dma, dma, dma, dma, dma, dma,
            pltpu.SemaphoreType.REGULAR((columns - 1,)), pltpu.SemaphoreType.REGULAR,
            pltpu.SemaphoreType.REGULAR,
        ],
        compiler_params=pltpu.CompilerParams(
            collective_id=0, has_side_effects=True, vmem_limit_bytes=44 << 20
        ),
    )(here(lengths), moves, *map(here, arrays))


def solution(mesh):
    placed = (
        P(None, "grp", "head", None),
        P(None, "grp", "head", None),
        P("head", None, None),
        P("head", None, None),
        P(("grp", "head"), None, None),
        P(None, ("grp", "head"), None),
        P(),
        P("head", None),
    )
    return jax.shard_map(
        body, mesh=mesh, in_specs=placed, out_specs=P(None, "grp", "head", None), check_vma=False
    )
```

```python
import functools
import math

import jax
import jax.numpy as jnp
from jax import lax
from jax.experimental import pallas as pl
from jax.experimental.pallas import tpu as pltpu
from jax.sharding import PartitionSpec as P

PAIR = 2
EXTRA = 128
LANES = 128
YARN_GAIN = (0.1 * math.log(40.0) + 1.0) ** 2
MESH = pl.DeviceIdType.MESH


def lane(c):
    return slice(c * LANES, (c + 1) * LANES)


def rounded(value):
    return value.astype(jnp.bfloat16)


def wide(value):
    return value.astype(jnp.float32)


def kernel(
    groups, columns, scale,
    length_hbm, move_ref, nope_hbm, rope_hbm, fresh_hbm, wk_hbm, wv_hbm, cache_hbm,
    out_ref,
    length_ref, nope_ref, rope_ref, fresh_ref, entry_sem,
    wk, wv, keys, newer, local_sem,
    rows_in, rows_mid, rows_out,
    lat_send, lat_recv, late_send, late_recv, rot_send, rot_recv, back_send, back_recv,
    mine, moved, mine_key, moved_key, home, home_recv, shift_of, shift_mine,
    lat_ss, lat_rs, late_ss, late_rs, rot_ss, rot_rs, back_ss, back_rs,
    mine_ss, mine_rs, key_ss, key_rs, home_ss, home_rs, shift_ss, shift_rs,
    near_sem, rank_sem, open_sem,
):
    steps, _, heads, _ = nope_ref.shape
    holders, entries, capacity = cache_hbm.shape
    latent = wk.shape[2]
    rope = entries - latent
    movers = move_ref.shape[1]
    total = capacity + EXTRA
    cuts = cuts_of(heads)
    cut = heads // cuts
    rank = lax.axis_index("grp")
    column = lax.axis_index("head")
    parts = wk.shape[0] // local_part(heads)
    part = local_part(heads)

    first = [(0, k) for k in range(holders)]
    rest = [(1, k) for k in range(movers, holders)]
    moving = [(1, k) for k in range(movers)]
    settled = first + rest
    number = {member: u for u, member in enumerate(settled + moving)}

    def at_column(e):
        return (rank, lax.rem(column + e + columns, columns))

    def at_group(d):
        return (lax.rem(rank + d + groups, groups), column)

    wk_copies = [
        pltpu.make_async_copy(
            wk_hbm.at[pl.ds(n * part, part)], wk.at[pl.ds(n * part, part)], local_sem.at[n]
        )
        for n in range(parts)
    ]
    key_copy = pltpu.make_async_copy(cache_hbm, keys, local_sem.at[parts])
    wv_copy = pltpu.make_async_copy(wv_hbm, wv, local_sem.at[parts + 1])
    entry_copies = [
        pltpu.make_async_copy(src, dst, entry_sem.at[n])
        for n, (src, dst) in enumerate(
            (
                (rope_hbm, rope_ref), (nope_hbm, nope_ref), (fresh_hbm, fresh_ref),
                (length_hbm, length_ref),
            )
        )
    ]
    for copy in entry_copies[:2] + wk_copies[:1]:
        copy.start()

    barrier = pltpu.get_barrier_semaphore()
    for e in range(1, columns):
        @pl.when(column + e < columns)
        def _():
            pl.semaphore_signal(barrier, inc=1, device_id=at_column(e), device_id_type=MESH)

    @pl.when(rank == 0)
    def _():
        for d in range(1, groups):
            pl.semaphore_signal(barrier, inc=1, device_id=at_group(d), device_id_type=MESH)

    below = column + jnp.minimum(rank, 1)

    @pl.when(below > 0)
    def _():
        pl.semaphore_wait(barrier, below)

    for e in range(1, columns):
        @pl.when(column >= e)
        def _():
            pl.semaphore_signal(
                near_sem.at[e - 1], inc=1, device_id=at_column(-e), device_id_type=MESH
            )

    @pl.when(rank > 0)
    def _():
        pl.semaphore_signal(rank_sem, inc=1, device_id=(0, column), device_id_type=MESH)

    def remote(src, dst, send, recv, target):
        return pltpu.make_async_remote_copy(
            src_ref=src, dst_ref=dst, send_sem=send, recv_sem=recv,
            device_id=target, device_id_type=MESH,
        )

    def slot(e, k):
        return lax.rem(column + e, columns) * holders + k

    def turned(span, e, k):
        return jnp.concatenate(
            [rope_ref[span * PAIR + s, slot(e, k)] for s in range(PAIR)], axis=1
        )

    def shift_copy(e):
        return remote(shift_mine, shift_of.at[columns - e], shift_ss, shift_rs, at_column(e))

    def mine_copy(d):
        return remote(mine, moved.at[d - 1], mine_ss, mine_rs, at_group(-d))

    def newer_copy(d):
        return remote(mine_key, moved_key.at[d - 1], key_ss, key_rs, at_group(-d))

    def home_copy(d):
        return remote(home, home_recv.at[d - 1], home_ss, home_rs, at_group(d))

    per = PAIR * cut
    joined = max(cuts - 2, 0)
    others = pl.ds(1, columns - 1)
    halves = [(0, cuts - 1), (cuts - 1, cuts)] if cuts > 1 else [(0, 1)]
    back_pieces = {member: [(0, cuts)] for member in number}
    if cuts > 1:
        for member in rest:
            back_pieces[member] = halves

    def rows_of(piece):
        return pl.ds(piece[0] * per, (piece[1] - piece[0]) * per)

    def lat_copy(e, c):
        at = pl.ds(c, cuts - c) if c == joined else pl.ds(c, 1)
        return remote(lat_send.at[e, at], lat_recv.at[e, at], lat_ss, lat_rs, at_column(e))

    def late_copy(e):
        return remote(late_send.at[e], late_recv.at[e], late_ss, late_rs, at_column(e))

    lats = remote(lat_send.at[others], lat_recv.at[others], lat_ss, lat_rs, at_column(1))
    lates = remote(late_send.at[others], late_recv.at[others], late_ss, late_rs, at_column(1))

    def rot_copy(late, e):
        at = pl.ds(len(settled), len(moving)) if late else pl.ds(0, len(settled))
        return remote(
            rot_send.at[e, at], rot_recv.at[e, at], rot_ss, rot_rs.at[late], at_column(e)
        )

    landed = {}
    for member in settled + moving:
        for c in range(len(back_pieces[member])):
            landed[member, c] = len(landed)

    def back_copy(member, e, c):
        u = number[member]
        at = rows_of(back_pieces[member][c])
        return remote(
            back_send.at[u, e, at], back_recv.at[u, e, at], back_ss,
            back_rs.at[landed[member, c]], at_column(-e),
        )

    def back_all(member, c):
        u = number[member]
        at = rows_of(back_pieces[member][c])
        return remote(
            back_send.at[u, others, at], back_recv.at[u, others, at], back_ss,
            back_rs.at[landed[member, c]], at_column(1),
        )

    low, high = jnp.int32(0), jnp.int32(columns - 1)
    near = []
    for _ in range(columns - 1):
        above, below = high - column, column - low
        take_high = jnp.where(2 * column < columns, above >= below, above > below)
        near.insert(0, jnp.where(take_high, high, low))
        high = jnp.where(take_high, high - 1, high)
        low = jnp.where(take_high, low, low + 1)
    near_up = [lax.rem(target - column + columns, columns) for target in near]
    near_down = [lax.rem(column - target + columns, columns) for target in near]

    far_down = near_down[::-1]
    end = jnp.logical_or(column == 0, column == columns - 1)

    def send_back(pieces, order):
        for member, c in pieces:
            for e in order:
                back_copy(member, e, c).start()

    def pieces_of(members, table):
        return [(member, c) for member in members for c in range(len(table[member]))]

    def chosen(e, k, options):
        found = wide(options(0))
        for d in range(2, groups):
            is_it = shift_of[e, k, 0:1, 0:1] == d
            found = jnp.where(is_it, wide(options(d - 1)), found)
        return found

    unit_rows = columns * PAIR * heads

    def place(m, e, s):
        return ((m * columns + e) * PAIR + s) * heads

    def turn(members, late):
        for span, k in members:
            u = number[span, k]
            for e in range(columns):
                if late:
                    pair = rounded(chosen(e, k, lambda n: moved[n, k, PAIR, e]))
                else:
                    pair = turned(span, e, k)
                if e:
                    rot_send[e, u] = pair
                else:
                    rot_recv[0, u] = pair

    def absorb(members, late, after):
        count = len(members) * columns * PAIR
        for m, (span, k) in enumerate(members):
            for e in range(columns):
                for s in range(PAIR):
                    if late:
                        value = chosen(e, k, lambda n: moved[n, k, s, e])
                    else:
                        value = wide(nope_ref[span * PAIR + s, slot(e, k)])
                    rows_in[pl.ds(place(m, e, s), heads)] = value
        for n in range(parts):
            if not late:
                wk_copies[n].wait()

            def head(i, carry):
                picked = rounded(rows_in[pl.ds(i, count, stride=heads)])
                result = jnp.dot(picked, wk[i], preferred_element_type=jnp.float32)
                for c in range(latent // LANES):
                    rows_mid[c, pl.ds(i, count, stride=heads)] = result[:, lane(c)]
                return carry

            lax.fori_loop(n * part, (n + 1) * part, head, 0, unroll=True)
            if (n + 1) % (parts // cuts):
                continue
            c = n // (parts // cuts)
            for m, member in enumerate(members):
                u = number[member]
                for e in range(columns):
                    value = rounded(
                        jnp.concatenate(
                            [
                                jnp.concatenate(
                                    [
                                        rows_mid[l, pl.ds(place(m, e, s) + c * cut, cut)]
                                        for l in range(latent // LANES)
                                    ],
                                    axis=1,
                                )
                                for s in range(PAIR)
                            ],
                            axis=0,
                        )
                    )
                    if late:
                        to, at = (late_send if e else late_recv), (e, m, c)
                    else:
                        to, at = (lat_send if e else lat_recv), (e, c, m)
                    to[at] = value
            after(c)

    entry_copies[0].wait()
    for copy in wk_copies[1:] + entry_copies[2:]:
        copy.start()
    turn(settled, 0)
    for k in range(movers):
        shift_mine[k] = jnp.full(shift_mine.shape[1:], move_ref[0, k], jnp.int32)
        shift_of[0, k] = jnp.full(shift_mine.shape[1:], move_ref[0, k], jnp.int32)
    for e in range(1, columns):
        @pl.when(column + e >= columns)
        def _():
            rot_copy(0, e).start()
            shift_copy(e).start()

    entry_copies[1].wait()
    row = lax.broadcasted_iota(jnp.int32, (16, entries), 0)

    def fresh_rows(k):
        found = jnp.zeros((16, entries), jnp.float32)
        for j in range(steps):
            found = jnp.where(row == j, wide(fresh_ref[j])[k : k + 1], found)
        return found

    def after_settled(c):
        ready = [j for j in ([joined] if c == cuts - 1 else [c]) if j < joined or c == cuts - 1]
        for e in range(1, columns):
            @pl.when(column + e >= columns)
            def _():
                for j in ready:
                    lat_copy(e, j).start()

            if c == 0:
                @pl.when(column + e < columns)
                def _():
                    pl.semaphore_wait(near_sem.at[e - 1], 1)
                    rot_copy(0, e).start()
                    shift_copy(e).start()

        for e in range(1, columns):
            @pl.when(column + e < columns)
            def _():
                for j in ready:
                    lat_copy(e, j).start()

        if c == 0:
            for copy in entry_copies[2:]:
                copy.wait()
            for k in range(movers):
                for e in range(columns):
                    for s in range(PAIR):
                        mine[k, s, e] = nope_ref[PAIR + s, slot(e, k)]
                    mine[k, PAIR, e] = turned(1, e, k)
                mine_key[k] = rounded(fresh_rows(k))

        if c == cuts - 1:
            @pl.when(rank == 0)
            def _():
                pl.semaphore_wait(rank_sem, groups - 1)
                for d in range(1, groups):
                    pl.semaphore_signal(
                        open_sem, inc=1, device_id=at_group(d), device_id_type=MESH
                    )

            @pl.when(rank > 0)
            def _():
                pl.semaphore_wait(open_sem, 1)

            for d in range(1, groups):
                mine_copy(d).start()
            for d in range(1, groups):
                newer_copy(d).start()

    absorb(settled, 0, after_settled)
    key_copy.start()
    wv_copy.start()
    for k in range(holders):
        newer[k] = jnp.zeros((EXTRA, entries), jnp.bfloat16)
        newer[k, 0:16] = rounded(fresh_rows(k))
    key_copy.wait()

    at_key = lax.broadcasted_iota(jnp.int32, (1, total), 1)
    at_row = lax.broadcasted_iota(jnp.int32, (unit_rows, 1), 0)
    within = lax.rem(lax.div(at_row, cut), PAIR)
    turns_in = set()

    def attend(member):
        span, k = member
        u = number[member]
        late = int(member in moving)
        if late not in turns_in:
            (lates if late else lats).wait_recv()
        if late not in turns_in:
            at = pl.ds(len(settled), len(moving)) if late else pl.ds(0, len(settled))
            remote(
                rot_send.at[others, at], rot_recv.at[others, at], rot_ss, rot_rs.at[late],
                at_column(1),
            ).wait_recv()
        turns_in.add(late)
        live = length_ref[(rank * columns + column) * holders + k]
        token = jnp.where(at_key < capacity, steps, at_key - capacity)
        token = jnp.where(at_key < live, -1, token)
        nt = (((1,), (1,)), ((), ()))
        queries = (late_recv[:, u - len(settled)] if late else lat_recv[:, :, u]).reshape(
            unit_rows, latent
        )
        pairs = [wide(rot_recv[e, u]) for e in range(columns)]
        turns = rounded(
            jnp.concatenate(
                [
                    pairs[e][c * cut : (c + 1) * cut, s * rope : (s + 1) * rope]
                    for e in range(columns)
                    for c in range(cuts)
                    for s in range(PAIR)
                ],
                axis=0,
            )
        )
        cached = jnp.dot(
            queries, keys[k, :latent], preferred_element_type=jnp.float32
        ) + jnp.dot(turns, keys[k, latent:], preferred_element_type=jnp.float32)
        decoded = lax.dot_general(
            queries, newer[k, :, :latent], nt, preferred_element_type=jnp.float32
        ) + lax.dot_general(
            turns, newer[k, :, latent:], nt, preferred_element_type=jnp.float32
        )
        scores = jnp.concatenate([cached, decoded], axis=1)
        scores = jnp.where(token <= span * PAIR + within, scores * scale, -jnp.inf)
        spread = jnp.exp(scores - jnp.max(scores, axis=1, keepdims=True))
        weights = rounded(spread * (1.0 / jnp.sum(spread, axis=1, keepdims=True)))
        mixed = rounded(
            lax.dot_general(
                weights[:, :capacity], keys[k, :latent], nt, preferred_element_type=jnp.float32
            )
            + jnp.dot(
                weights[:, capacity:], newer[k, :, :latent], preferred_element_type=jnp.float32
            )
        ).reshape(columns, PAIR * heads, latent)
        back_recv[u, 0] = mixed[0]
        for e in range(1, columns):
            back_send[u, e] = mixed[e]

    def project(member, c):
        span, k = member
        u = number[member]
        low, high = back_pieces[member][c] if c is not None else (0, cuts)
        for j in range(len(back_pieces[member])) if c is None else [c]:
            back_all(member, j).wait_recv()
        for e in range(columns):
            for j in range(low, high):
                value = wide(back_recv[u, e, j * per : (j + 1) * per])
                for s in range(PAIR):
                    for l in range(latent // LANES):
                        rows_mid[l, pl.ds(place(0, e, s) + j * cut, cut)] = value[
                            s * cut : (s + 1) * cut, lane(l)
                        ]

        def head(i, carry):
            at = pl.ds(i, columns * PAIR, stride=heads)
            picked = jnp.concatenate(
                [rounded(rows_mid[l, at]) for l in range(latent // LANES)], axis=1
            )
            rows_out[at] = jnp.dot(picked, wv[i], preferred_element_type=jnp.float32)
            return carry

        count = (high - low) * cut
        start = low * cut
        lax.fori_loop(start, start + count, head, 0, unroll=True)
        for e in range(columns):
            for s in range(PAIR):
                value = rounded(rows_out[pl.ds(place(0, e, s) + start, count)])
                if member in moving:
                    home[k, s, e, start : start + count] = value
                else:
                    out_ref[span * PAIR + s, slot(e, k), start : start + count] = value

    shifts = remote(shift_of.at[others], shift_of.at[others], shift_ss, shift_rs, at_column(1))
    mines = remote(moved, moved, mine_ss, mine_rs, at_group(1))
    newers = remote(moved_key, moved_key, key_ss, key_rs, at_group(1))
    homes = remote(home_recv, home_recv, home_ss, home_rs, at_group(1))
    for copy in (shifts, mines):
        copy.wait_recv()
    turn(moving, 1)
    for e in near_up:
        rot_copy(1, e).start()
    absorb(moving, 1, lambda c: None)
    for e in near_up:
        late_copy(e).start()
    attend(first[0])

    @pl.when(jnp.logical_not(end))
    def _():
        send_back(pieces_of(first[:1], back_pieces), far_down)

    newers.wait_recv()
    for k in range(movers):
        later = chosen(0, k, lambda n: moved_key[n, k])
        newer[k, 0:16] = rounded(jnp.where(row < PAIR, wide(newer[k, 0:16]), later))
    for member in moving:
        attend(member)
    send_back(pieces_of(moving, back_pieces), far_down)

    @pl.when(end)
    def _():
        send_back(pieces_of(first[:1], back_pieces), far_down)

    for member in settled[1:]:
        attend(member)
    odd = lax.rem(rank, 2) == 1
    past = [jnp.where(odd, a, b) for a, b in zip(near_down[1:], far_down[:-1])]
    send_back(pieces_of(settled[1:], back_pieces), near_down[:1])
    upper = jnp.logical_and(2 * column >= columns, jnp.logical_not(odd))

    @pl.when(upper)
    def _():
        for e in past:
            send_back(pieces_of(settled[1:], back_pieces), [e])

    @pl.when(jnp.logical_not(upper))
    def _():
        send_back(pieces_of(first[1:], back_pieces), past)
        for e in past:
            send_back(pieces_of(rest, back_pieces), [e])
    wv_copy.wait()
    for member in moving:
        project(member, None)
    for d in range(1, groups):
        home_copy(d).start()
    for member in first:
        project(member, None)
    for c in range(len(halves)):
        for member in rest:
            project(member, c)
    homes.wait_recv()
    for k in range(movers):
        for e in range(columns):
            for s in range(PAIR):
                out_ref[PAIR + s, slot(e, k)] = rounded(
                    chosen(e, k, lambda n: home_recv[n, k, s, e])
                )
    remote(
        rot_send.at[others], rot_recv.at[others], rot_ss, rot_rs.at[0], at_column(1)
    ).wait_send()
    remote(
        back_send.at[:, others], back_recv.at[:, others], back_ss, back_rs.at[0], at_column(1)
    ).wait_send()
    for copy in (lats, lates, shifts, mines, newers, homes):
        copy.wait_send()


def local_part(heads):
    return max(heads // 4, 1)


def cuts_of(heads):
    return 1 if heads % 32 else 4


def body(q_nope, q_rope, w_absorb_k, w_absorb_v, latent_cache, new_latent, lengths, moves):
    steps, slots, heads, width = q_nope.shape
    rope = q_rope.shape[3]
    latent = w_absorb_k.shape[2]
    holders, capacity, entries = latent_cache.shape
    movers = moves.shape[1]
    groups = lax.axis_size("grp")
    columns = lax.axis_size("head")
    scale = YARN_GAIN / math.sqrt(width + rope)
    assert steps == 2 * PAIR
    units = steps // PAIR * holders
    rows = (2 * holders - movers) * columns * PAIR * heads
    others = groups - 1
    bf16, f32 = jnp.bfloat16, jnp.float32
    dma = pltpu.SemaphoreType.DMA
    hbm = pl.BlockSpec(memory_space=pl.ANY)
    parts = heads // local_part(heads)
    cuts = cuts_of(heads)
    here = functools.partial(pltpu.with_memory_space_constraint, memory_space=pltpu.HBM)
    arrays = (
        q_nope, q_rope, new_latent, w_absorb_k, w_absorb_v, jnp.swapaxes(latent_cache, 1, 2)
    )
    return pl.pallas_call(
        functools.partial(kernel, groups, columns, scale),
        out_shape=pltpu.VMEM(q_nope.shape, bf16),
        in_specs=[hbm, pl.BlockSpec(memory_space=pltpu.SMEM)] + [hbm] * len(arrays),
        out_specs=pl.BlockSpec(memory_space=pltpu.VMEM),
        scratch_shapes=[
            pltpu.SMEM(lengths.shape, jnp.int32),
            pltpu.VMEM(q_nope.shape, bf16),
            pltpu.VMEM(q_rope.shape, bf16),
            pltpu.VMEM(new_latent.shape, bf16),
            dma((4,)),
            pltpu.VMEM(w_absorb_k.shape, bf16),
            pltpu.VMEM(w_absorb_v.shape, bf16),
            pltpu.VMEM((holders, entries, capacity), bf16),
            pltpu.VMEM((holders, EXTRA, entries), bf16),
            dma((parts + 2,)),
            pltpu.VMEM((rows, width), f32),
            pltpu.VMEM((latent // LANES, rows, LANES), f32),
            pltpu.VMEM((rows, width), f32),
            pltpu.VMEM((columns, cuts, units - movers, PAIR * heads // cuts, latent), bf16),
            pltpu.VMEM((columns, cuts, units - movers, PAIR * heads // cuts, latent), bf16),
            pltpu.VMEM((columns, movers, cuts, PAIR * heads // cuts, latent), bf16),
            pltpu.VMEM((columns, movers, cuts, PAIR * heads // cuts, latent), bf16),
            pltpu.VMEM((columns, units, heads, PAIR * rope), bf16),
            pltpu.VMEM((columns, units, heads, PAIR * rope), bf16),
            pltpu.VMEM((units, columns, PAIR * heads, latent), bf16),
            pltpu.VMEM((units, columns, PAIR * heads, latent), bf16),
            pltpu.VMEM((movers, PAIR + 1, columns, heads, width), bf16),
            pltpu.VMEM((others, movers, PAIR + 1, columns, heads, width), bf16),
            pltpu.VMEM((movers, 16, entries), bf16),
            pltpu.VMEM((others, movers, 16, entries), bf16),
            pltpu.VMEM((movers, PAIR, columns, heads, width), bf16),
            pltpu.VMEM((others, movers, PAIR, columns, heads, width), bf16),
            pltpu.VMEM((columns, movers, 8, LANES), jnp.int32),
            pltpu.VMEM((movers, 8, LANES), jnp.int32),
            dma, dma, dma, dma,
            dma, dma((2,)),
            dma, dma((2 * units,)),
            dma, dma, dma, dma, dma, dma, dma, dma,
            pltpu.SemaphoreType.REGULAR((columns - 1,)), pltpu.SemaphoreType.REGULAR,
            pltpu.SemaphoreType.REGULAR,
        ],
        compiler_params=pltpu.CompilerParams(
            collective_id=0, has_side_effects=True, vmem_limit_bytes=44 << 20
        ),
    )(here(lengths), moves, *map(here, arrays))


def solution(mesh):
    placed = (
        P(None, "grp", "head", None),
        P(None, "grp", "head", None),
        P("head", None, None),
        P("head", None, None),
        P(("grp", "head"), None, None),
        P(None, ("grp", "head"), None),
        P(),
        P("head", None),
    )
    return jax.shard_map(
        body, mesh=mesh, in_specs=placed, out_specs=P(None, "grp", "head", None), check_vma=False
    )
```
